32 devices in a mesh: grp: 2 (over y), roll: 4 (over z), head: 2 (over x), sub: 2 (over core).
Axes of the slice: x: 2, y: 2, z: 4, core: 2. Of those that a mesh axis runs over, the one named last changes fastest.
Arguments:
- queries: bfloat16 [16, 256, 32, 128], P(('grp', 'roll', 'sub'), None, 'head'), parts along dimension 0, may hold values from -16 to 16
- rollout_keys: bfloat16 [16, 256, 8, 128], P(('grp', 'roll', 'sub'), None, 'head'), parts along dimension 0, may hold values from -6 to 6
- rollout_values: bfloat16 [16, 256, 8, 128], P(('grp', 'roll', 'sub'), None, 'head'), parts along dimension 0, may hold values from -6 to 6
- prefix_keys: bfloat16 [1280, 8, 128], P(('grp', 'roll', 'sub'), 'head'), parts along dimension 0, may hold values from -6 to 6
- audio_prefix_values: bfloat16 [1280, 8, 128], P(('grp', 'roll', 'sub'), 'head'), parts along dimension 0, may hold values from -6 to 6
- lengths: int32 [16], P(('grp', 'roll', 'sub')), parts along dimension 0, may hold values from 1 to 256, 1152 in all
- grad_out: bfloat16 [16, 256, 32, 128], P(('grp', 'roll', 'sub'), None, 'head'), parts along dimension 0, may hold values from -96 to 96
Outputs:
- grad_queries: bfloat16 [16, 256, 32, 128], P(('grp', 'roll', 'sub'), None, 'head'), parts along dimension 0
- grad_self_keys: bfloat16 [16, 256, 8, 128], P(('grp', 'roll', 'sub'), None, 'head'), parts along dimension 0
- grad_self_values: bfloat16 [16, 256, 8, 128], P(('grp', 'roll', 'sub'), None, 'head'), parts along dimension 0
- grad_prefix_keys: bfloat16 [1280, 8, 128], P(('grp', 'roll', 'sub'), 'head'), parts along dimension 0
- grad_prefix_values: bfloat16 [1280, 8, 128], P(('grp', 'roll', 'sub'), 'head'), parts along dimension 0
The draws below stay inside these ranges and needn't reach their ends.
There are 2 independent parts, one for each index of `grp`. The reference program is written for one: setup_inputs(seed, part) draws one part's arguments, and reference() takes and returns one part's arrays. A program takes and returns all parts, laid end to end along the dimension named above; each array names one. Nothing has to cross between parts.
Inputs may be any that keep to these rules, and one draw needn't show every extreme that they name: `lengths`: some rollout has exactly 256 live tokens in every draw.
All inputs are finite; a program needn't handle non-finite values. No bound on the sum of `lengths` on one device may be relied on, other than what follows from the above.
Results may differ from the reference program's by a relative error of at most 0.0054.
Values may be sent and summed in bfloat16 or wider, within the bound.
A program may use at most 64 MiB of HBM per device.

```python
import math
import jax
import jax.numpy as jnp
import numpy as np
from jax import lax

QUERY_HEAD_COUNT = 32
KEY_VALUE_HEADS = 8
HEAD_SIZE = 128
ROLLOUT_LENGTH = 256
ROLLOUT_COUNT = 8
PREFIX_TOKENS = 640


def draw_queries(key, part):
    full_shape = (ROLLOUT_COUNT, ROLLOUT_LENGTH, QUERY_HEAD_COUNT, HEAD_SIZE)
    values = jnp.clip(jax.random.normal(jax.random.fold_in(key, 4), full_shape, jnp.float32), -6.0, 6.0)
    return values.astype(jnp.bfloat16)


def draw_prefix_keys(key, part):
    full_shape = (PREFIX_TOKENS, KEY_VALUE_HEADS, HEAD_SIZE)
    values = jnp.clip(jax.random.normal(jax.random.fold_in(key, 7), full_shape, jnp.float32), -6.0, 6.0)
    return values.astype(jnp.bfloat16)


def levels(key, dims, cuts, smallest, top_value):
    gain, own = 1.0, jax.random.fold_in(key, 6)
    for axis_at, blocks in cuts:
        heights = jnp.exp(jax.random.uniform(jax.random.fold_in(own, axis_at), (blocks,), jnp.float32, smallest / len(cuts), top_value / len(cuts)))
        gain = gain * jnp.repeat(heights, dims[axis_at] // blocks).reshape([-1 if axis == axis_at else 1 for axis in range(len(dims))])
    return gain


def profile(number_of, total, most, skew):
    weights = [(1 << 20) // math.isqrt(standing ** skew) + 1 for standing in range(2, number_of + 1)]
    spare, given = total - most - (number_of - 1), [1] * (number_of - 1)
    while spare > 0:
        candidates = [i for i in range(number_of - 1) if given[i] < most]
        whole, budget = sum([weights[i] for i in candidates]), spare
        for i in candidates:
            more = min(most - given[i], max(1, budget * weights[i] // whole), spare)
            given[i] = given[i] + more
            spare = spare - more
    return np.array([most] + given)


def uneven(key, count, total, most, skew):
    if count == 2:
        one = jax.random.randint(key, (), max(1, total - most), min(most, total - 1) + 1)
        return jnp.stack([one, total - one])
    sizes = jnp.asarray(profile(count, total, most, skew), jnp.int32)
    twos = (count - 1) // 2
    source_of, taker = sizes[1:1 + 2 * twos:2], sizes[2:2 + 2 * twos:2]
    margin = jnp.minimum(source_of - 1, most - taker)
    passed = jax.random.randint(jax.random.fold_in(key, 1), (twos,), 0, 1 << 20) % (margin + 1)
    sizes = sizes.at[1:1 + 2 * twos:2].set(source_of - passed).at[2:2 + 2 * twos:2].set(taker + passed)
    return sizes[jax.random.permutation(jax.random.fold_in(key, 2), count)]


def noise(rng, shape, deviation, bound, split=(), kind=jnp.bfloat16):
    result = jax.random.normal(rng, shape, jnp.float32) * deviation
    if len(split) > 0:
        result = levels(rng, shape, split, -0.22, 0.18) * result
    return jnp.clip(result, min=-bound, max=bound).astype(kind)


def setup_inputs(seed: int = 0, part: int = 0) -> dict:
    keys = jax.random.split(jax.random.key(seed), 8)
    own_keys = jax.random.split(jax.random.fold_in(keys[7], part), 8)
    return {
        "queries": draw_queries(jax.random.fold_in(jax.random.fold_in(keys[7], part), 71), part),
        "rollout_keys": noise(own_keys[1], (ROLLOUT_COUNT, ROLLOUT_LENGTH, KEY_VALUE_HEADS, HEAD_SIZE), 1.0, 6.0, ((0, 8), (2, 2))),
        "rollout_values": noise(own_keys[2], (ROLLOUT_COUNT, ROLLOUT_LENGTH, KEY_VALUE_HEADS, HEAD_SIZE), 1.0, 6.0, ((0, 8), (2, 2))),
        "prefix_keys": draw_prefix_keys(jax.random.fold_in(jax.random.fold_in(keys[7], part), 71), part),
        "audio_prefix_values": noise(own_keys[4], (PREFIX_TOKENS, KEY_VALUE_HEADS, HEAD_SIZE), 1.0, 6.0, ((0, 8), (1, 2))),
        "lengths": uneven(own_keys[5], ROLLOUT_COUNT, ROLLOUT_COUNT * ROLLOUT_LENGTH // 2 + ROLLOUT_LENGTH // 2, ROLLOUT_LENGTH, 2).astype(jnp.int32),
        "grad_out": noise(own_keys[6], (ROLLOUT_COUNT, ROLLOUT_LENGTH, QUERY_HEAD_COUNT, HEAD_SIZE), 16.0, 96.0, ((0, 8), (2, 2))),
    }


masked_score = -1e+30

def rollout_grads(query_row_block, own_key, own_value, output_gradient, length, prefix_keys, audio_prefix_values):
    longest_token_length = query_row_block.shape[0]
    query_group_width = QUERY_HEAD_COUNT // KEY_VALUE_HEADS
    inv_root = 1.0 / math.sqrt(HEAD_SIZE)
    positions = jnp.arange(longest_token_length, dtype=jnp.int32)
    live = positions < length
    output_gradient = jnp.where(live[:, None, None], output_gradient, jnp.zeros_like(output_gradient))
    query_by_group = query_row_block.reshape(longest_token_length, KEY_VALUE_HEADS, query_group_width, HEAD_SIZE).astype(jnp.float32)
    output_gradient_grouped = output_gradient.reshape(longest_token_length, KEY_VALUE_HEADS, query_group_width, HEAD_SIZE).astype(jnp.float32)
    all_keys = jnp.concatenate([prefix_keys, own_key], axis=0).astype(jnp.float32)
    all_values = jnp.concatenate([audio_prefix_values, own_value], axis=0).astype(jnp.float32)
    key_index = jnp.arange(PREFIX_TOKENS + longest_token_length, dtype=jnp.int32)
    allowed = (key_index[None, :] < PREFIX_TOKENS) | (key_index[None, :] - PREFIX_TOKENS <= positions[:, None])
    scores = jnp.einsum('lkgd,pkd->kglp', query_by_group, all_keys) * inv_root
    scores = jnp.where(allowed, scores, masked_score)
    row_top = lax.optimization_barrier(jnp.max(scores, axis=-1, keepdims=True))
    log_total = row_top + jnp.log(lax.optimization_barrier(jnp.sum(jnp.exp(scores - row_top), axis=-1, keepdims=True)))
    weights = jnp.exp(scores - log_total)
    dweights = jnp.einsum('lkgd,pkd->kglp', output_gradient_grouped, all_values)
    row_inner = lax.optimization_barrier(jnp.sum(weights * dweights, axis=-1, keepdims=True))
    rounded_weights = lax.optimization_barrier(weights.astype(jnp.bfloat16)).astype(jnp.float32)
    score_gradient = lax.optimization_barrier((inv_root * weights * (dweights - row_inner)).astype(jnp.bfloat16)).astype(jnp.float32)
    grad_query = jnp.einsum('kglp,pkd->lkgd', score_gradient, all_keys).reshape(longest_token_length, QUERY_HEAD_COUNT, HEAD_SIZE).astype(jnp.bfloat16)
    grad_keys = jnp.einsum('kglp,lkgd->pkd', score_gradient, query_by_group)
    grad_values = jnp.einsum('kglp,lkgd->pkd', rounded_weights, output_gradient_grouped)
    return (grad_query, grad_keys[PREFIX_TOKENS:].astype(jnp.bfloat16), grad_values[PREFIX_TOKENS:].astype(jnp.bfloat16), grad_keys[:PREFIX_TOKENS], grad_values[:PREFIX_TOKENS])

def reference(queries, rollout_keys, rollout_values, prefix_keys, audio_prefix_values, lengths, grad_out):

    def advance(totals, inputs):
        results = rollout_grads(inputs[0], inputs[1], inputs[2], inputs[3], inputs[4], prefix_keys, audio_prefix_values)
        return ((totals[0] + results[3], totals[1] + results[4]), (results[0], results[1], results[2]))
    empty_sum_state = jnp.zeros((PREFIX_TOKENS, KEY_VALUE_HEADS, HEAD_SIZE), jnp.float32)
    totals, stacked = lax.scan(advance, (empty_sum_state, empty_sum_state), (queries, rollout_keys, rollout_values, grad_out, lengths))
    return (stacked[0], stacked[1], stacked[2], totals[0].astype(jnp.bfloat16), totals[1].astype(jnp.bfloat16))
```

```python
import functools
import math

import jax
import jax.numpy as jnp
from jax import lax
from jax.experimental import pallas as pl
from jax.experimental.pallas import tpu as pltpu
from jax.sharding import PartitionSpec as P

MESH = pl.DeviceIdType.MESH
VMEM_MIB = 56
LOG2E = math.log2(math.e)
F32 = jnp.float32
BF16 = jnp.bfloat16


def nt(a, b):
    return lax.dot_general(a, b, (((1,), (1,)), ((), ())), preferred_element_type=F32)


def nn(a, b):
    return lax.dot_general(a, b, (((1,), (0,)), ((), ())), preferred_element_type=F32)


def tn(a, b):
    return lax.dot_general(a, b, (((0,), (0,)), ((), ())), preferred_element_type=F32)


def swap(x):
    return jnp.transpose(x, (1, 0, 2))


def kernel(
    n_roll, n_sub,
    len_ref, q_in, ks_in, vs_in, pk_in, pv_in, do_in,
    dq_out, gks_out, gvs_out, gpk_out, gpv_out,
    q_ref, ks_ref, vs_ref, pk_ref, pv_ref, do_ref,
    dq_ref, gks_ref, gvs_ref, gpk_ref, gpv_ref,
    qt, dot, kvp, kvo, accp, acco, dqt, dqa, own, sbuf, rbuf, csum, rin,
    ag_send, ag_recv, al_send, al_recv, fw_send, fw_recv, pr_send, pr_recv, rs_send, rs_recv, in_sem, out_sem,
):
    z = lax.axis_index("roll")
    c = lax.axis_index("sub")
    other = 1 - c
    tokens, heads, width = q_ref.shape
    kv = ks_ref.shape[1]
    group = heads // kv
    part = pk_ref.shape[0]
    prefix = n_roll * n_sub * part
    inv_root = 1.0 / math.sqrt(width)

    barrier = pltpu.get_barrier_semaphore()
    for k in range(1, n_roll):
        pl.semaphore_signal(
            barrier, inc=1, device_id={"roll": lax.rem(z + k, n_roll)}, device_id_type=MESH
        )
    pl.semaphore_signal(barrier, inc=1, device_id={"sub": other}, device_id_type=MESH)

    ins = []
    for n, (src, dst) in enumerate((
        (pk_in, pk_ref), (pv_in, pv_ref), (q_in, q_ref), (do_in, do_ref), (ks_in, ks_ref), (vs_in, vs_ref),
    )):
        copy = pltpu.make_async_copy(src, dst, in_sem.at[n])
        copy.start()
        ins.append(copy)

    def put(src, dst, n):
        copy = pltpu.make_async_copy(src, dst, out_sem.at[n])
        copy.start()
        return copy

    ins[0].wait()
    pk_t = swap(pk_ref[...])
    ins[1].wait()
    pv_t = swap(pv_ref[...])
    for g in range(kv):
        kvp[g, 0, z, c] = pk_t[g]
        kvp[g, 1, z, c] = pv_t[g]
    pl.semaphore_wait(barrier, n_roll)

    def ag(g, k):
        mine = kvp.at[g, :, z, c]
        return pltpu.make_async_remote_copy(
            src_ref=mine, dst_ref=mine,
            send_sem=al_send.at[k], recv_sem=al_recv.at[k],
            device_id={"roll": lax.rem(z + k, n_roll)}, device_id_type=MESH,
        )

    def fw(g):
        column = kvp.at[g, :, :, c]
        return pltpu.make_async_remote_copy(
            src_ref=column, dst_ref=column,
            send_sem=fw_send.at[g], recv_sem=fw_recv.at[g],
            device_id={"sub": other}, device_id_type=MESH,
        )

    def pr(g):
        return pltpu.make_async_remote_copy(
            src_ref=sbuf.at[g], dst_ref=rbuf.at[g],
            send_sem=pr_send.at[g], recv_sem=pr_recv.at[g],
            device_id={"sub": other}, device_id_type=MESH,
        )

    def hop(g, at, right):
        block = kvp.at[g, :, at, c]
        return pltpu.make_async_remote_copy(
            src_ref=block, dst_ref=block,
            send_sem=ag_send.at[g, at, 0 if right else 1], recv_sem=ag_recv.at[g, at],
            device_id={"roll": z + 1 if right else z - 1}, device_id_type=MESH,
        )

    def pass_on(g, r):
        left, right = z - r + 1, z + r - 1

        @pl.when(left >= 0)
        def _():
            if r > 1:
                hop(g, left, True).wait_recv()

            @pl.when(z < n_roll - 1)
            def _():
                hop(g, left, True).start()

        @pl.when(right < n_roll)
        def _():
            if r > 1:
                hop(g, right, False).wait_recv()

            @pl.when(z > 0)
            def _():
                hop(g, right, False).start()

    def chain_end(g):
        r = n_roll

        @pl.when(z - r + 1 >= 0)
        def _():
            hop(g, z - r + 1, True).wait_recv()

        @pl.when(z + r - 1 < n_roll)
        def _():
            hop(g, z + r - 1, False).wait_recv()

        fw(g).start()

    def chain_sent(g):
        for at in range(n_roll):
            @pl.when((z >= at) & (z < n_roll - 1))
            def _():
                hop(g, at, True).wait_send()

            @pl.when((z <= at) & (z > 0))
            def _():
                hop(g, at, False).wait_send()

    def step_sum(g, to, slot, right):
        return pltpu.make_async_remote_copy(
            src_ref=csum.at[g, to], dst_ref=rin.at[g, slot],
            send_sem=rs_send.at[g, to], recv_sem=rs_recv.at[g, slot],
            device_id={"roll": z + 1 if right else z - 1}, device_id_type=MESH,
        )

    def sum_on(g, r):
        for right in (True, False):
            to = z + n_roll - r if right else z + r - n_roll
            first = z == 0 if right else z == n_roll - 1
            sends = (to <= n_roll - 1) if right else (to >= 0)

            @pl.when(sends & first)
            def _():
                for i in range(2):
                    csum[g, to, i] = (accp[g, i, to, c] + rbuf[g, i, to].astype(F32)).astype(BF16)

            @pl.when(sends & jnp.logical_not(first))
            def _():
                step_sum(g, to, to, right).wait_recv()
                for i in range(2):
                    csum[g, to, i] = (
                        accp[g, i, to, c] + rbuf[g, i, to].astype(F32) + rin[g, to, i].astype(F32)
                    ).astype(BF16)

            @pl.when(sends)
            def _():
                if right:
                    slot = to
                else:
                    slot = jnp.where(to == z - 1, n_roll, to)
                step_sum(g, to, slot, right).start()

    def sums_sent(g):
        for to in range(n_roll):
            @pl.when(z != to)
            def _():
                step_sum(g, to, to, True).wait_send()

    def rs(g, k):
        to = lax.rem(z + k, n_roll)
        return pltpu.make_async_remote_copy(
            src_ref=csum.at[g, to], dst_ref=rin.at[g, k],
            send_sem=rs_send.at[g, k], recv_sem=rs_recv.at[g, k],
            device_id={"roll": to}, device_id_type=MESH,
        )

    def offer(g):
        for k in range(1, n_roll):
            ag(g, k).start()

    rounds = list(range(1, n_roll))
    third = (len(rounds) + 2) // 3
    phases = (rounds[:third], rounds[third:2 * third], rounds[2 * third:])

    def pass_phase(g, phase):
        for r in phases[phase]:
            pass_on(g, r)

    def sum_phase(g, phase):
        for r in phases[phase]:
            sum_on(g, r)

    offer(0)
    if kv > 1:
        pass_phase(1, 0)

    def forward(g):
        for k in range(1, n_roll):
            ag(g, k).wait_recv()
        fw(g).start()

    def spread(g):
        pr(g).wait_recv()
        for j in range(n_roll):
            for i in range(2):
                csum[g, j, i] = (accp[g, i, j, c] + rbuf[g, i, j].astype(F32)).astype(BF16)
        for k in range(1, n_roll):
            rs(g, k).start()

    length = len_ref[0]
    step = 16
    token_at = lax.broadcasted_iota(jnp.int32, (step, heads, width), 0)

    def turn(b, carry):
        at = pl.multiple_of(b * step, step)
        rows = pl.ds(at, step)
        qt[:, rows, :] = swap(q_ref[rows])
        raw = do_ref[rows].astype(F32)
        raw = jnp.where(token_at + at < length, raw, 0.0).astype(BF16)
        dot[:, rows, :] = swap(raw)
        return carry

    ins[2].wait()
    ins[3].wait()
    lax.fori_loop(0, tokens // step, turn, 0)
    ins[4].wait()
    ins[5].wait()
    ks_t = swap(ks_ref[...])
    vs_t = swap(vs_ref[...])
    kvo[:, 0] = ks_t
    kvo[:, 1] = vs_t
    accp[...] = jnp.zeros(accp.shape, F32)
    forward(0)
    if kv > 1:
        pass_phase(1, 1)

    key_at = lax.broadcasted_iota(jnp.int32, (tokens, tokens), 0)
    row_at = lax.broadcasted_iota(jnp.int32, (tokens, tokens), 1)

    scale = inv_root * LOG2E

    def rows_of(t, kp, vp, ko, vo):
        q = qt[t]
        do = dot[t]
        sp = nt(kp, q)
        so = jnp.where(key_at <= row_at, nt(ko, q), -1e30)
        top = jnp.maximum(
            jnp.max(sp, axis=0, keepdims=True), jnp.max(so, axis=0, keepdims=True)
        )
        ep = jnp.exp2((sp - top) * scale)
        eo = jnp.exp2((so - top) * scale)
        total = jnp.sum(ep, axis=0, keepdims=True) + jnp.sum(eo, axis=0, keepdims=True)
        dp = nt(vp, do)
        dw = nt(vo, do)
        inner = jnp.sum(ep * dp, axis=0, keepdims=True) + jnp.sum(eo * dw, axis=0, keepdims=True)
        inv = 1.0 / total
        delta = inner * inv
        wp = ep * inv
        wo = eo * inv
        gp = (wp * ((dp - delta) * inv_root)).astype(BF16)
        go = (wo * ((dw - delta) * inv_root)).astype(BF16)
        dqa[t] = tn(gp, kp)
        own[0, t] = go
        own[1, t] = wo.astype(BF16)
        return gp, wp.astype(BF16), q, do

    many = min(2, group)

    def advance(b, carry):
        t = b * many
        g = t // group
        r = t % group

        @pl.when(r == 0)
        def _():
            fw(g).wait_recv()

        kp = kvp[g, 0].reshape(prefix, width)
        vp = kvp[g, 1].reshape(prefix, width)
        ko = kvo[g, 0]
        vo = kvo[g, 1]
        done = [rows_of(t + m, kp, vp, ko, vo) for m in range(many)]
        for gp, wp, q, do in done:
            accp[g, 0] += nn(gp, q).reshape(n_roll, n_sub, part, width)
            accp[g, 1] += nn(wp, do).reshape(n_roll, n_sub, part, width)

        @pl.when((r == 0) & (g + 1 < kv))
        def _():
            pass_phase(g + 1, 2)

        @pl.when((r == 0) & (g + 2 < kv))
        def _():
            pass_phase(g + 2, 0)

        @pl.when((r == group - many) & (g + 2 < kv))
        def _():
            pass_phase(g + 2, 1)

        @pl.when((r == group - many) & (g + 1 < kv))
        def _():
            chain_end(g + 1)

        @pl.when((r == 0) & (g > 1))
        def _():
            sum_phase(g - 2, 2)

        @pl.when((r == 0) & (g > 0))
        def _():
            pr(g - 1).wait_recv()
            sum_phase(g - 1, 0)

        @pl.when((r == group - many) & (g > 0))
        def _():
            sum_phase(g - 1, 1)

        @pl.when(r == group - many)
        def _():
            for i in range(2):
                sbuf[g, i] = accp[g, i, :, other].astype(BF16)
            pr(g).start()

        return carry

    lax.fori_loop(0, heads // many, advance, 0)

    def turn_back(b, carry):
        rows = pl.ds(pl.multiple_of(b * step, step), step)
        dq_ref[rows] = swap(dqt[:, rows, :])
        return carry

    def own_grads(g, carry):
        ko = kvo[g, 0]
        grad_k = jnp.zeros((tokens, width), F32)
        grad_v = jnp.zeros((tokens, width), F32)
        for m in range(group):
            t = g * group + m
            go = own[0, t]
            dqt[t] = (dqa[t] + tn(go, ko)).astype(BF16)
            grad_k = grad_k + nn(go, qt[t])
            grad_v = grad_v + nn(own[1, t], dot[t])
        acco[0, g] = grad_k.astype(BF16)
        acco[1, g] = grad_v.astype(BF16)
        return carry

    half = kv // 2
    lax.fori_loop(0, half, own_grads, 0)
    spread(kv - 1)
    if kv > 1:
        sum_phase(kv - 2, 2)
    lax.fori_loop(half, kv, own_grads, 0)
    lax.fori_loop(0, tokens // step, turn_back, 0)
    outs = [put(dq_ref, dq_out, 0)]
    gks_ref[...] = swap(acco[0])
    gvs_ref[...] = swap(acco[1])
    outs.append(put(gks_ref, gks_out, 1))
    outs.append(put(gvs_ref, gvs_out, 2))
    for g in range(kv - 1):
        @pl.when(z > 0)
        def _():
            step_sum(g, z, z, True).wait_recv()
            for i in range(2):
                accp[g, i, z, c] += rin[g, z, i].astype(F32)

        @pl.when(z < n_roll - 1)
        def _():
            step_sum(g, z, n_roll, False).wait_recv()
            for i in range(2):
                accp[g, i, z, c] += rin[g, n_roll, i].astype(F32)

    for k in range(1, n_roll):
        rs(kv - 1, k).wait_recv()
        for i in range(2):
            accp[kv - 1, i, z, c] += rin[kv - 1, k, i].astype(F32)
    for i, out, hbm in ((0, gpk_ref, gpk_out), (1, gpv_ref, gpv_out)):
        mine = accp[:, i, z, c] + rbuf[:, i, z].astype(F32)
        out[...] = swap(mine.astype(BF16))
        outs.append(put(out, hbm, 3 + i))
    for copy in outs:
        copy.wait()
    for g in range(kv):
        fw(g).wait_send()
        pr(g).wait_send()
        if g > 0:
            chain_sent(g)
        if g < kv - 1:
            sums_sent(g)
    for k in range(1, n_roll):
        ag(0, k).wait_send()
        rs(kv - 1, k).wait_send()


def hand_on(*refs):
    held, came, went = refs[10:15], refs[15], refs[16]
    moves = []
    for n in range(5):
        copy = pltpu.make_async_copy(refs[n], held[n], came.at[n])
        copy.start()
        moves.append((copy, pltpu.make_async_copy(held[n], refs[5 + n], went.at[n])))
    for copy, onward in moves:
        copy.wait()
        onward.start()
    for copy, onward in moves:
        onward.wait()


def per_device(n_roll, n_sub, queries, rollout_keys, rollout_values, prefix_keys,
               audio_prefix_values, lengths, grad_out):
    here, tokens, heads, width = queries.shape
    kv = rollout_keys.shape[2]
    part = prefix_keys.shape[0]
    any_space = pl.BlockSpec(memory_space=pltpu.HBM)
    shapes = (
        (tokens, heads, width), (tokens, kv, width), (tokens, kv, width), (part, kv, width), (part, kv, width),
    )
    results = tuple(jax.ShapeDtypeStruct(shape, BF16) for shape in shapes)
    dma = pltpu.SemaphoreType.DMA
    outs = pl.pallas_call(
        functools.partial(kernel, n_roll, n_sub),
        out_shape=results,
        in_specs=[pl.BlockSpec(memory_space=pltpu.SMEM)] + [any_space] * 6,
        out_specs=(any_space,) * 5,
        scratch_shapes=[
            pltpu.VMEM(shapes[0], BF16), pltpu.VMEM(shapes[1], BF16), pltpu.VMEM(shapes[2], BF16),
            pltpu.VMEM(shapes[3], BF16), pltpu.VMEM(shapes[4], BF16), pltpu.VMEM(shapes[0], BF16),
            *[pltpu.VMEM(shape, BF16) for shape in shapes],
            pltpu.VMEM((heads, tokens, width), BF16),
            pltpu.VMEM((heads, tokens, width), BF16),
            pltpu.VMEM((kv, 2, n_roll, n_sub, part, width), BF16),
            pltpu.VMEM((kv, 2, tokens, width), BF16),
            pltpu.VMEM((kv, 2, n_roll, n_sub, part, width), F32),
            pltpu.VMEM((2, kv, tokens, width), BF16),
            pltpu.VMEM((heads, tokens, width), BF16),
            pltpu.VMEM((heads, tokens, width), F32),
            pltpu.VMEM((2, heads, tokens, tokens), BF16),
            pltpu.VMEM((kv, 2, n_roll, part, width), BF16),
            pltpu.VMEM((kv, 2, n_roll, part, width), BF16),
            pltpu.VMEM((kv, n_roll, 2, part, width), BF16),
            pltpu.VMEM((kv, n_roll + 1, 2, part, width), BF16),
            dma((kv, n_roll, 2)), dma((kv, n_roll)),
            dma((n_roll,)), dma((n_roll,)),
            dma((kv,)), dma((kv,)),
            dma((kv,)), dma((kv,)),
            dma((kv, n_roll)), dma((kv, n_roll + 1)),
            dma((6,)), dma((5,)),
        ],
        compiler_params=pltpu.CompilerParams(
            collective_id=0, has_side_effects=True, vmem_limit_bytes=VMEM_MIB * 1024 * 1024
        ),
    )(lengths, queries[0], rollout_keys[0], rollout_values[0], prefix_keys,
      audio_prefix_values, grad_out[0])
    outs = pl.pallas_call(
        hand_on,
        out_shape=results,
        in_specs=[any_space] * 5,
        out_specs=(any_space,) * 5,
        scratch_shapes=[*[pltpu.VMEM(shape, BF16) for shape in shapes], dma((5,)), dma((5,))],
    )(*outs)
    return outs[0][None], outs[1][None], outs[2][None], outs[3], outs[4]


def solution(mesh):
    rows = P(("grp", "roll", "sub"), None, "head", None)
    pieces = P(("grp", "roll", "sub"), "head", None)
    return jax.shard_map(
        functools.partial(per_device, mesh.shape["roll"], mesh.shape["sub"]),
        mesh=mesh,
        in_specs=(rows, rows, rows, pieces, pieces, P(("grp", "roll", "sub")), rows),
        out_specs=(rows, rows, rows, pieces, pieces),
        check_vma=False,
    )
```

```python
import functools
import math

import jax
import jax.numpy as jnp
from jax import lax
from jax.experimental import pallas as pl
from jax.experimental.pallas import tpu as pltpu
from jax.sharding import PartitionSpec as P

MESH = pl.DeviceIdType.MESH
VMEM_MIB = 56
LOG2E = math.log2(math.e)
F32 = jnp.float32
BF16 = jnp.bfloat16


def nt(a, b):
    return lax.dot_general(a, b, (((1,), (1,)), ((), ())), preferred_element_type=F32)


def nn(a, b):
    return lax.dot_general(a, b, (((1,), (0,)), ((), ())), preferred_element_type=F32)


def tn(a, b):
    return lax.dot_general(a, b, (((0,), (0,)), ((), ())), preferred_element_type=F32)


def swap(x):
    return jnp.transpose(x, (1, 0, 2))


def kernel(
    n_roll, n_sub,
    len_ref, q_in, ks_in, vs_in, pk_in, pv_in, do_in,
    dq_ref, gks_ref, gvs_ref, gpk_ref, gpv_ref,
    q_ref, ks_ref, vs_ref, pk_ref, pv_ref, do_ref,
    qt, dot, kvp, kvo, accp, acco, dqt, es, ds, gw, eo, wo, so, ga, wa, sbuf, rbuf, csum, rin, rina,
    ag_send, ag_recv, al_send, fw_send, fw_recv, pr_send, pr_recv, rs_send, rs_recv, ra_send, ra_recv, in_sem,
):
    z = lax.axis_index("roll")
    c = lax.axis_index("sub")
    other = 1 - c
    tokens, heads, width = q_ref.shape
    kv = ks_ref.shape[1]
    group = heads // kv
    part = pk_ref.shape[0]
    prefix = n_roll * n_sub * part
    inv_root = 1.0 / math.sqrt(width)

    barrier = pltpu.get_barrier_semaphore()
    for k in range(1, n_roll):
        pl.semaphore_signal(
            barrier, inc=1, device_id={"roll": lax.rem(z + k, n_roll)}, device_id_type=MESH
        )
    pl.semaphore_signal(barrier, inc=1, device_id={"sub": other}, device_id_type=MESH)

    ins = []
    for n, (src, dst) in enumerate((
        (pk_in, pk_ref), (pv_in, pv_ref), (q_in, q_ref), (do_in, do_ref), (ks_in, ks_ref), (vs_in, vs_ref),
    )):
        copy = pltpu.make_async_copy(src, dst, in_sem.at[n])
        copy.start()
        ins.append(copy)

    ins[0].wait()
    pk_t = swap(pk_ref[...])
    ins[1].wait()
    pv_t = swap(pv_ref[...])
    for g in range(kv):
        kvp[g, 0, z, c] = pk_t[g]
        kvp[g, 1, z, c] = pv_t[g]
    pl.semaphore_wait(barrier, n_roll)

    def later(g, first, act):
        if isinstance(g, int):
            if g > first:
                act(g - 1)
        else:
            pl.when(g > first)(lambda: act(g - 1))

    def ag(k):
        mine = kvp.at[0, :, z, c]
        return pltpu.make_async_remote_copy(
            src_ref=mine, dst_ref=mine,
            send_sem=al_send.at[k - 1], recv_sem=ag_recv.at[0, z],
            device_id={"roll": lax.rem(z + k, n_roll)}, device_id_type=MESH,
        )

    def send_block(g, at, to, n):
        block = kvp.at[g, :, at, c]
        return pltpu.make_async_remote_copy(
            src_ref=block, dst_ref=block,
            send_sem=ag_send.at[n], recv_sem=ag_recv.at[g, at],
            device_id={"roll": to}, device_id_type=MESH,
        )

    def each_hop(g, act):
        @pl.when(z > 0)
        def _():
            act(send_block(g, z, z - 1, n_roll))

        @pl.when(z < n_roll - 1)
        def _():
            act(send_block(g, z, z + 1, n_roll + 1))

    def each_relay(g, act):
        for to in range(n_roll):
            @pl.when((z >= 1) & (to > z))
            def _():
                act(send_block(g, z - 1, to, to))

            @pl.when((z <= n_roll - 2) & (to < z))
            def _():
                act(send_block(g, z + 1, to, to))

    def landed(g, at):
        send_block(g, at, z, 0).wait_recv()

    def hop(g):
        later(g, 1, lambda h: each_hop(h, lambda copy: copy.wait_send()))
        each_hop(g, lambda copy: copy.start())
        share(g, z)

    def relay(g):
        @pl.when(z > 0)
        def _():
            landed(g, z - 1)

        @pl.when(z < n_roll - 1)
        def _():
            landed(g, z + 1)

        later(g, 1, lambda h: each_relay(h, lambda copy: copy.wait_send()))
        each_relay(g, lambda copy: copy.start())

        @pl.when(z > 0)
        def _():
            share(g, z - 1)

        @pl.when(z < n_roll - 1)
        def _():
            share(g, z + 1)

    def finish(g):
        for at in range(n_roll):
            @pl.when((z > at + 1) | (z < at - 1))
            def _():
                landed(g, at)
                share(g, at)

    def fw(g, at):
        block = kvp.at[g, :, at, c]
        return pltpu.make_async_remote_copy(
            src_ref=block, dst_ref=block,
            send_sem=fw_send.at[at], recv_sem=fw_recv.at[g],
            device_id={"sub": other}, device_id_type=MESH,
        )

    def share(g, at):
        later(g, 0, lambda h: fw(h, at).wait_send())
        fw(g, at).start()

    def shared(g):
        column = kvp.at[g, :, :, c]
        pltpu.make_async_remote_copy(
            src_ref=column, dst_ref=column,
            send_sem=fw_send.at[0], recv_sem=fw_recv.at[g],
            device_id={"sub": other}, device_id_type=MESH,
        ).wait_recv()

    def pr(g):
        return pltpu.make_async_remote_copy(
            src_ref=sbuf.at[g], dst_ref=rbuf.at[g],
            send_sem=pr_send, recv_sem=pr_recv.at[g],
            device_id={"sub": other}, device_id_type=MESH,
        )

    mate = z + 1 - 2 * lax.rem(z, 2)
    side = lax.rem(z, 2)

    def near(g, j):
        return pltpu.make_async_remote_copy(
            src_ref=csum.at[g, 2 * j + 1 - side], dst_ref=rina.at[g, j],
            send_sem=ra_send.at[j], recv_sem=ra_recv.at[g],
            device_id={"roll": mate}, device_id_type=MESH,
        )

    def far(g, k):
        to = lax.rem(z + 2 * k, n_roll)
        return pltpu.make_async_remote_copy(
            src_ref=csum.at[g, to], dst_ref=rin.at[g, k],
            send_sem=rs_send.at[k], recv_sem=rs_recv.at[g, k],
            device_id={"roll": to}, device_id_type=MESH,
        )

    def round_a(g):
        pr(g).wait_recv()
        for j in range(n_roll // 2):
            at = 2 * j + 1 - side
            for i in range(2):
                csum[g, at, i] = (accp[g, i, at, c] + rbuf[g, i, at].astype(F32)).astype(BF16)
            later(g, 0, lambda h: near(h, j).wait_send())
            near(g, j).start()

    def round_b(g):
        pltpu.make_async_remote_copy(
            src_ref=rina.at[g], dst_ref=rina.at[g],
            send_sem=ra_send.at[0], recv_sem=ra_recv.at[g],
            device_id={"roll": mate}, device_id_type=MESH,
        ).wait_recv()
        for k in range(1, n_roll // 2):
            at = lax.rem(z + 2 * k, n_roll)
            for i in range(2):
                csum[g, at, i] = (
                    accp[g, i, at, c] + rbuf[g, i, at].astype(F32) + rina[g, at // 2, i].astype(F32)
                ).astype(BF16)
            later(g, 0, lambda h: far(h, k).wait_send())
            far(g, k).start()

    for k in range(1, n_roll):
        ag(k).start()
    share(0, z)

    def forward():
        for k in range(1, n_roll):
            at = lax.rem(z + n_roll - k, n_roll)
            landed(0, at)
            share(0, at)

    length = len_ref[0]
    step = 16
    token_at = lax.broadcasted_iota(jnp.int32, (step, heads, width), 0)

    def turn(b, carry):
        at = pl.multiple_of(b * step, step)
        rows = pl.ds(at, step)
        qt[:, rows, :] = swap(q_ref[rows])
        raw = do_ref[rows].astype(F32)
        raw = jnp.where(token_at + at < length, raw, 0.0).astype(BF16)
        dot[:, rows, :] = swap(raw)
        return carry

    ins[2].wait()
    ins[3].wait()
    lax.fori_loop(0, tokens // step, turn, 0)
    ins[4].wait()
    ins[5].wait()
    ks_t = swap(ks_ref[...])
    vs_t = swap(vs_ref[...])
    kvo[:, 0] = ks_t
    kvo[:, 1] = vs_t
    accp[...] = jnp.zeros(accp.shape, F32)

    key_at = lax.broadcasted_iota(jnp.int32, (128, tokens), 0)
    row_at = lax.broadcasted_iota(jnp.int32, (128, tokens), 1)

    scale = inv_root * LOG2E

    tile = 128
    tiles_p = prefix // tile
    tiles_o = tokens // tile

    def tile_stats(s, dp):
        top = jnp.max(s, axis=0, keepdims=True)
        e = jnp.exp2((s - top) * scale)
        return e, top, jnp.sum(e, axis=0, keepdims=True), jnp.sum(e * dp, axis=0, keepdims=True)

    def own_scores(b, carry):
        for m in range(2):
            t = 2 * b + m
            g = t // group
            q, do = qt[t], dot[t]
            ko, vo = kvo[g, 0], kvo[g, 1]
            for n in range(tiles_o):
                at = slice(n * tile, (n + 1) * tile)
                s = jnp.where(key_at + n * tile <= row_at, nt(ko[at], q), -1e30)
                dp = nt(vo[at], do)
                e, top, total, inner = tile_stats(s, dp)
                eo[t, at] = e
                wo[t, at] = dp
                so[t, n, 0] = top
                so[t, n, 1] = total
                so[t, n, 2] = inner
        return carry

    def weigh(t, slot):
        g = t // group
        q, do = qt[t], dot[t]
        kp = kvp[g, 0].reshape(prefix, width)
        vp = kvp[g, 1].reshape(prefix, width)
        tops, sums, inners = [], [], []
        for n in range(tiles_p):
            at = slice(n * tile, (n + 1) * tile)
            dp = nt(vp[at], do)
            e, top, total, inner = tile_stats(nt(kp[at], q), dp)
            es[slot, at] = e
            ds[slot, at] = dp
            tops.append(top)
            sums.append(total)
            inners.append(inner)
        for n in range(tiles_o):
            tops.append(so[t, n, 0])
            sums.append(so[t, n, 1])
            inners.append(so[t, n, 2])
        most = functools.reduce(jnp.maximum, tops)
        parts = [jnp.exp2((top - most) * scale) for top in tops]
        total = sum(p * x for p, x in zip(parts, sums))
        inner = sum(p * x for p, x in zip(parts, inners))
        inv = 1.0 / total
        delta = inner * inv
        for n in range(tiles_p):
            at = slice(n * tile, (n + 1) * tile)
            w = es[slot, at] * (parts[n] * inv)
            gp = (w * (ds[slot, at] - delta)).astype(BF16)
            gw[slot, 0, at] = gp
            gw[slot, 1, at] = w.astype(BF16)
            ga[t, at] = gp
        for n in range(tiles_o):
            at = slice(n * tile, (n + 1) * tile)
            w = eo[t, at] * (parts[tiles_p + n] * inv)
            ga[t, prefix + n * tile:prefix + (n + 1) * tile] = (w * (wo[t, at] - delta)).astype(BF16)
            wa[t, at] = w.astype(BF16)

    def collect(t, slot):
        g = t // group
        accp[g, 0] += nn(gw[slot, 0], qt[t]).reshape(n_roll, n_sub, part, width)
        accp[g, 1] += nn(gw[slot, 1], dot[t]).reshape(n_roll, n_sub, part, width)

    def late(g, carry):
        kp = kvp[g, 0].reshape(prefix, width)
        ko = kvo[g, 0]
        grad_k = jnp.zeros((tokens, width), F32)
        grad_v = jnp.zeros((tokens, width), F32)
        for m in range(group):
            t = g * group + m
            go = ga[t, prefix:]
            dqt[t] = ((tn(ga[t, :prefix], kp) + tn(go, ko)) * inv_root).astype(BF16)
            grad_k = grad_k + nn(go, qt[t])
            grad_v = grad_v + nn(wa[t], dot[t])
        acco[0, g] = (grad_k * inv_root).astype(BF16)
        acco[1, g] = grad_v.astype(BF16)
        return carry

    many = 2

    def start_pair(g):
        for i in range(2):
            sbuf[g, i] = accp[g, i, :, other].astype(BF16)
        later(g, 0, lambda h: pr(h).wait_send())
        pr(g).start()

    lax.fori_loop(0, heads // 4, own_scores, 0)
    if kv > 1:
        hop(1)
    lax.fori_loop(heads // 4, heads // 2, own_scores, 0)
    forward()
    if kv > 2:
        hop(2)
    if kv > 1:
        relay(1)
    if kv > 3:
        hop(3)

    def advance(b, carry):
        t = b * many
        g = t // group
        r = t % group

        @pl.when(r == 0)
        def _():
            shared(g)

        weigh(t, 0)
        weigh(t + 1, 1)
        collect(t, 0)
        collect(t + 1, 1)

        if kv > 1:
            @pl.when((r == group - many) & (g == 0))
            def _():
                finish(1)

        @pl.when(b + 2 < kv)
        def _():
            relay(b + 2)

        @pl.when(b + 4 < kv)
        def _():
            hop(b + 4)

        @pl.when((r == 0) & (g > 0) & (g + 1 < kv))
        def _():
            finish(g + 1)

        @pl.when((r == 0) & (g > 0))
        def _():
            round_a(g - 1)

        @pl.when((r == group - many) & (g > 1))
        def _():
            round_b(g - 2)

        @pl.when(r == group - many)
        def _():
            start_pair(g)

        return carry

    lax.fori_loop(0, heads // many, advance, 0)

    def turn_back(b, carry):
        rows = pl.ds(pl.multiple_of(b * step, step), step)
        dq_ref[rows] = swap(dqt[:, rows, :])
        return carry

    lax.fori_loop(0, kv // 4, late, 0)
    round_a(kv - 1)
    lax.fori_loop(kv // 4, kv // 2, late, 0)
    lax.fori_loop(kv // 2, 3 * kv // 4, late, 0)
    if kv > 1:
        round_b(kv - 2)
    lax.fori_loop(3 * kv // 4, kv, late, 0)
    lax.fori_loop(0, tokens // step, turn_back, 0)
    round_b(kv - 1)
    gks_ref[...] = swap(acco[0])
    gvs_ref[...] = swap(acco[1])
    for g in range(kv):
        for i in range(2):
            accp[g, i, z, c] += rbuf[g, i, z].astype(F32)
        for i in range(2):
            accp[g, i, z, c] += rina[g, z // 2, i].astype(F32)
        for k in range(1, n_roll // 2):
            far(g, k).wait_recv()
            for i in range(2):
                accp[g, i, z, c] += rin[g, k, i].astype(F32)
    for i, out in ((0, gpk_ref), (1, gpv_ref)):
        mine = accp[:, i, z, c]
        out[...] = swap((mine * inv_root if i == 0 else mine).astype(BF16))
    last = kv - 1
    pr(last).wait_send()
    for at in range(n_roll):
        fw(last, at).wait_send()
    if kv > 1:
        each_hop(last, lambda copy: copy.wait_send())
        each_relay(last, lambda copy: copy.wait_send())
    for j in range(n_roll // 2):
        near(last, j).wait_send()
    for k in range(1, n_roll // 2):
        far(last, k).wait_send()
    for k in range(1, n_roll):
        ag(k).wait_send()


def hand_on(*refs):
    moves = [pltpu.make_async_copy(refs[n], refs[5 + n], refs[10].at[n]) for n in range(5)]
    for copy in moves:
        copy.start()
    for copy in moves:
        copy.wait()


def per_device(n_roll, n_sub, queries, rollout_keys, rollout_values, prefix_keys,
               audio_prefix_values, lengths, grad_out):
    here, tokens, heads, width = queries.shape
    kv = rollout_keys.shape[2]
    part = prefix_keys.shape[0]
    prefix = n_roll * n_sub * part
    any_space = pl.BlockSpec(memory_space=pltpu.HBM)
    shapes = (
        (tokens, heads, width), (tokens, kv, width), (tokens, kv, width), (part, kv, width), (part, kv, width),
    )
    results = tuple(jax.ShapeDtypeStruct(shape, BF16) for shape in shapes)
    dma = pltpu.SemaphoreType.DMA
    outs = pl.pallas_call(
        functools.partial(kernel, n_roll, n_sub),
        out_shape=tuple(pltpu.VMEM(shape, BF16) for shape in shapes),
        in_specs=[pl.BlockSpec(memory_space=pltpu.SMEM)] + [any_space] * 6,
        out_specs=(pl.BlockSpec(memory_space=pltpu.VMEM),) * 5,
        scratch_shapes=[
            pltpu.VMEM(shapes[0], BF16), pltpu.VMEM(shapes[1], BF16), pltpu.VMEM(shapes[2], BF16),
            pltpu.VMEM(shapes[3], BF16), pltpu.VMEM(shapes[4], BF16), pltpu.VMEM(shapes[0], BF16),
            pltpu.VMEM((heads, tokens, width), BF16),
            pltpu.VMEM((heads, tokens, width), BF16),
            pltpu.VMEM((kv, 2, n_roll, n_sub, part, width), BF16),
            pltpu.VMEM((kv, 2, tokens, width), BF16),
            pltpu.VMEM((kv, 2, n_roll, n_sub, part, width), F32),
            pltpu.VMEM((2, kv, tokens, width), BF16),
            pltpu.VMEM((heads, tokens, width), BF16),
            pltpu.VMEM((2, prefix, tokens), F32),
            pltpu.VMEM((2, prefix, tokens), F32),
            pltpu.VMEM((2, 2, prefix, tokens), BF16),
            pltpu.VMEM((heads, tokens, tokens), F32),
            pltpu.VMEM((heads, tokens, tokens), F32),
            pltpu.VMEM((heads, tokens // 128, 3, 1, tokens), F32),
            pltpu.VMEM((heads, prefix + tokens, tokens), BF16),
            pltpu.VMEM((heads, tokens, tokens), BF16),
            pltpu.VMEM((kv, 2, n_roll, part, width), BF16),
            pltpu.VMEM((kv, 2, n_roll, part, width), BF16),
            pltpu.VMEM((kv, n_roll, 2, part, width), BF16),
            pltpu.VMEM((kv, n_roll, 2, part, width), BF16),
            pltpu.VMEM((kv, n_roll // 2, 2, part, width), BF16),
            dma((n_roll + 2,)), dma((kv, n_roll)), dma((n_roll - 1,)),
            dma((n_roll,)), dma((kv,)),
            dma, dma((kv,)),
            dma((n_roll // 2,)), dma((kv, n_roll // 2)),
            dma((n_roll // 2,)), dma((kv,)),
            dma((6,)),
        ],
        compiler_params=pltpu.CompilerParams(
            collective_id=0, has_side_effects=True, vmem_limit_bytes=VMEM_MIB * 1024 * 1024
        ),
    )(lengths, queries[0], rollout_keys[0], rollout_values[0], prefix_keys,
      audio_prefix_values, grad_out[0])
    outs = pl.pallas_call(
        hand_on,
        out_shape=results,
        in_specs=[pl.BlockSpec(memory_space=pltpu.VMEM)] * 5,
        out_specs=(any_space,) * 5,
        scratch_shapes=[dma((5,))],
    )(*[pltpu.with_memory_space_constraint(out, pltpu.VMEM) for out in outs])
    return outs[0][None], outs[1][None], outs[2][None], outs[3], outs[4]


def solution(mesh):
    rows = P(("grp", "roll", "sub"), None, "head", None)
    pieces = P(("grp", "roll", "sub"), "head", None)
    return jax.shard_map(
        functools.partial(per_device, mesh.shape["roll"], mesh.shape["sub"]),
        mesh=mesh,
        in_specs=(rows, rows, rows, pieces, pieces, P(("grp", "roll", "sub")), rows),
        out_specs=(rows, rows, rows, pieces, pieces),
        check_vma=False,
    )
```

```python
import functools
import math

import jax
import jax.numpy as jnp
from jax import lax
from jax.experimental import pallas as pl
from jax.experimental.pallas import tpu as pltpu
from jax.sharding import PartitionSpec as P

MESH = pl.DeviceIdType.MESH
VMEM_MIB = 56
LOG2E = math.log2(math.e)
F32 = jnp.float32
BF16 = jnp.bfloat16


def nt(a, b):
    return lax.dot_general(a, b, (((1,), (1,)), ((), ())), preferred_element_type=F32)


def nn(a, b):
    return lax.dot_general(a, b, (((1,), (0,)), ((), ())), preferred_element_type=F32)


def tn(a, b):
    return lax.dot_general(a, b, (((0,), (0,)), ((), ())), preferred_element_type=F32)


def swap(x):
    return jnp.transpose(x, (1, 0, 2))


def kernel(
    n_roll, n_sub,
    len_ref, q_in, ks_in, vs_in, pk_in, pv_in, do_in,
    dq_ref, gks_ref, gvs_ref, gpk_ref, gpv_ref,
    q_ref, ks_ref, vs_ref, pk_ref, pv_ref, do_ref,
    qt, dot, kvp, kvo, accp, acco, dqt, es, ds, gw, eo, wo, so, ga, wa, sbuf, rbuf, csum, rin, rina,
    al_send, hop_send, relay_send, ag_recv, fw_send, fw_recv, pr_send, pr_recv, rs_send, rs_recv, ra_send, ra_recv, in_sem,
):
    z = lax.axis_index("roll")
    c = lax.axis_index("sub")
    other = 1 - c
    tokens, heads, width = q_ref.shape
    kv = ks_ref.shape[1]
    group = heads // kv
    part = pk_ref.shape[0]
    prefix = n_roll * n_sub * part
    inv_root = 1.0 / math.sqrt(width)

    barrier = pltpu.get_barrier_semaphore()
    for k in range(1, n_roll):
        pl.semaphore_signal(
            barrier, inc=1, device_id={"roll": lax.rem(z + k, n_roll)}, device_id_type=MESH
        )
    pl.semaphore_signal(barrier, inc=1, device_id={"sub": other}, device_id_type=MESH)

    ins = []
    for n, (src, dst) in enumerate((
        (pk_in, pk_ref), (pv_in, pv_ref), (q_in, q_ref), (do_in, do_ref), (ks_in, ks_ref), (vs_in, vs_ref),
    )):
        copy = pltpu.make_async_copy(src, dst, in_sem.at[n])
        copy.start()
        ins.append(copy)

    ins[0].wait()
    pk_t = swap(pk_ref[...])
    ins[1].wait()
    pv_t = swap(pv_ref[...])
    for g in range(kv):
        kvp[g, z, c, 0] = pk_t[g]
        kvp[g, z, c, 1] = pv_t[g]
    pl.semaphore_wait(barrier, n_roll)

    def ag(k):
        mine = kvp.at[0, z, c]
        return pltpu.make_async_remote_copy(
            src_ref=mine, dst_ref=mine,
            send_sem=al_send, recv_sem=ag_recv.at[0, z],
            device_id={"roll": lax.rem(z + k, n_roll)}, device_id_type=MESH,
        )

    def send_block(g, at, to, sem):
        block = kvp.at[g, at, c]
        return pltpu.make_async_remote_copy(
            src_ref=block, dst_ref=block,
            send_sem=sem, recv_sem=ag_recv.at[g, at],
            device_id={"roll": to}, device_id_type=MESH,
        )

    def all_sent(sent, sem):
        pltpu.make_async_remote_copy(
            src_ref=sent, dst_ref=sent, send_sem=sem, recv_sem=ag_recv.at[0, 0],
            device_id={"sub": other}, device_id_type=MESH,
        ).wait_send()

    def landed(g, at):
        send_block(g, at, z, al_send).wait_recv()

    def hop(g):
        @pl.when(z > 0)
        def _():
            send_block(g, z, z - 1, hop_send).start()

        @pl.when(z < n_roll - 1)
        def _():
            send_block(g, z, z + 1, hop_send).start()

        share(g, z)

    def relay(g):
        @pl.when(z > 0)
        def _():
            landed(g, z - 1)

        @pl.when(z < n_roll - 1)
        def _():
            landed(g, z + 1)

        for to in range(n_roll):
            @pl.when((z >= 1) & (to > z))
            def _():
                send_block(g, z - 1, to, relay_send).start()

            @pl.when((z <= n_roll - 2) & (to < z))
            def _():
                send_block(g, z + 1, to, relay_send).start()

        @pl.when(z > 0)
        def _():
            share(g, z - 1)

        @pl.when(z < n_roll - 1)
        def _():
            share(g, z + 1)

    def finish(g):
        for at in range(n_roll):
            @pl.when((z > at + 1) | (z < at - 1))
            def _():
                landed(g, at)
                share(g, at)

    def fw(g, at):
        block = kvp.at[g, at, c]
        return pltpu.make_async_remote_copy(
            src_ref=block, dst_ref=block,
            send_sem=fw_send, recv_sem=fw_recv.at[g],
            device_id={"sub": other}, device_id_type=MESH,
        )

    def share(g, at):
        fw(g, at).start()

    def shared(g):
        column = kvp.at[g, :, c]
        pltpu.make_async_remote_copy(
            src_ref=column, dst_ref=column,
            send_sem=fw_send, recv_sem=fw_recv.at[g],
            device_id={"sub": other}, device_id_type=MESH,
        ).wait_recv()

    def pr(g):
        return pltpu.make_async_remote_copy(
            src_ref=sbuf.at[g], dst_ref=rbuf.at[g],
            send_sem=pr_send, recv_sem=pr_recv.at[g],
            device_id={"sub": other}, device_id_type=MESH,
        )

    mate = z + 1 - 2 * lax.rem(z, 2)
    side = lax.rem(z, 2)

    def near(g, j):
        return pltpu.make_async_remote_copy(
            src_ref=csum.at[g, 2 * j + 1 - side], dst_ref=rina.at[g, j],
            send_sem=ra_send, recv_sem=ra_recv.at[g, j],
            device_id={"roll": mate}, device_id_type=MESH,
        )

    def far(g, k):
        to = lax.rem(z + 2 * k, n_roll)
        return pltpu.make_async_remote_copy(
            src_ref=csum.at[g, to], dst_ref=rin.at[g, k],
            send_sem=rs_send, recv_sem=rs_recv.at[g, k - 1],
            device_id={"roll": to}, device_id_type=MESH,
        )

    def round_a(g):
        pr(g).wait_recv()
        for n in range(1, n_roll // 2 + 1):
            j = lax.rem(z // 2 + n, n_roll // 2)
            at = 2 * j + 1 - side
            for i in range(2):
                csum[g, at, i] = (accp[g, i, at, c] + rbuf[g, i, at].astype(F32)).astype(BF16)
            near(g, j).start()

    def round_b(g):
        for n in range(1, n_roll // 2):
            near(g, lax.rem(z // 2 + n, n_roll // 2)).wait_recv()
        for k in range(1, n_roll // 2):
            at = lax.rem(z + 2 * k, n_roll)
            for i in range(2):
                csum[g, at, i] = (
                    accp[g, i, at, c] + rbuf[g, i, at].astype(F32) + rina[g, at // 2, i].astype(F32)
                ).astype(BF16)
            far(g, k).start()

    for k in range(1, n_roll):
        ag(k).start()
    share(0, z)

    def forward():
        for k in range(1, n_roll):
            at = lax.rem(z + n_roll - k, n_roll)
            landed(0, at)
            share(0, at)

    length = len_ref[0]
    step = 16
    token_at = lax.broadcasted_iota(jnp.int32, (step, heads, width), 0)

    def turn(b, carry):
        at = pl.multiple_of(b * step, step)
        rows = pl.ds(at, step)
        qt[:, rows, :] = swap(q_ref[rows])
        raw = do_ref[rows].astype(F32)
        raw = jnp.where(token_at + at < length, raw, 0.0).astype(BF16)
        dot[:, rows, :] = swap(raw)
        return carry

    ins[2].wait()
    ins[3].wait()
    lax.fori_loop(0, tokens // step, turn, 0)
    ins[4].wait()
    ins[5].wait()
    ks_t = swap(ks_ref[...])
    vs_t = swap(vs_ref[...])
    kvo[:, 0] = ks_t
    kvo[:, 1] = vs_t
    accp[...] = jnp.zeros(accp.shape, F32)

    key_at = lax.broadcasted_iota(jnp.int32, (128, tokens), 0)
    row_at = lax.broadcasted_iota(jnp.int32, (128, tokens), 1)

    scale = inv_root * LOG2E

    tile = 128
    tiles_p = prefix // tile
    tiles_o = tokens // tile

    def tile_stats(s, dp):
        top = jnp.max(s, axis=0, keepdims=True)
        e = jnp.exp2((s - top) * scale)
        return e, top, jnp.sum(e, axis=0, keepdims=True), jnp.sum(e * dp, axis=0, keepdims=True)

    def own_scores(b, carry):
        for m in range(2):
            t = 2 * b + m
            g = t // group
            do = dot[t]
            q = qt[t]
            ko, vo = kvo[g, 0], kvo[g, 1]
            for n in range(tiles_o):
                at = slice(n * tile, (n + 1) * tile)
                s = jnp.where(key_at + n * tile <= row_at, nt(ko[at], q), -1e30)
                dp = nt(vo[at], do)
                e, top, total, inner = tile_stats(s, dp)
                eo[t, at] = e
                wo[t, at] = dp
                so[t, n, 0] = top
                so[t, n, 1] = total
                so[t, n, 2] = inner
        return carry

    def weigh(t, slot):
        g = t // group
        q, do = qt[t], dot[t]
        kp = kvp[g, :, :, 0].reshape(prefix, width)
        vp = kvp[g, :, :, 1].reshape(prefix, width)
        tops, sums, inners = [], [], []
        for n in range(tiles_p):
            at = slice(n * tile, (n + 1) * tile)
            dp = nt(vp[at], do)
            e, top, total, inner = tile_stats(nt(kp[at], q), dp)
            es[slot, at] = e
            ds[slot, at] = dp
            tops.append(top)
            sums.append(total)
            inners.append(inner)
        for n in range(tiles_o):
            tops.append(so[t, n, 0])
            sums.append(so[t, n, 1])
            inners.append(so[t, n, 2])
        most = functools.reduce(jnp.maximum, tops)
        parts = [jnp.exp2((top - most) * scale) for top in tops]
        total = sum(p * x for p, x in zip(parts, sums))
        inner = sum(p * x for p, x in zip(parts, inners))
        inv = 1.0 / total
        delta = inner * inv
        for n in range(tiles_p):
            at = slice(n * tile, (n + 1) * tile)
            w = es[slot, at] * (parts[n] * inv)
            gp = (w * (ds[slot, at] - delta)).astype(BF16)
            ga[t, at] = gp
            gw[slot, at] = w.astype(BF16)
        for n in range(tiles_o):
            so[t, n, 0] = parts[tiles_p + n] * inv
        so[t, 0, 1] = delta

    def collect(t, slot):
        g = t // group
        accp[g, 0] += nn(ga[t, :prefix], qt[t]).reshape(n_roll, n_sub, part, width)
        accp[g, 1] += nn(gw[slot], dot[t]).reshape(n_roll, n_sub, part, width)

    def late(g, carry):
        kp = kvp[g, :, :, 0].reshape(prefix, width)
        ko = kvo[g, 0]
        grad_k = jnp.zeros((tokens, width), F32)
        grad_v = jnp.zeros((tokens, width), F32)
        for m in range(group):
            t = g * group + m
            delta = so[t, 0, 1]
            for n in range(tiles_o):
                at = slice(n * tile, (n + 1) * tile)
                w = eo[t, at] * so[t, n, 0]
                ga[t, prefix + n * tile:prefix + (n + 1) * tile] = (w * (wo[t, at] - delta)).astype(BF16)
                wa[t, at] = w.astype(BF16)
            go = ga[t, prefix:]
            dqt[t] = ((tn(ga[t, :prefix], kp) + tn(go, ko)) * inv_root).astype(BF16)
            grad_k = grad_k + nn(go, qt[t])
            grad_v = grad_v + nn(wa[t], dot[t])
        acco[0, g] = (grad_k * inv_root).astype(BF16)
        acco[1, g] = grad_v.astype(BF16)
        return carry

    many = 2

    def start_pair(g):
        for i in range(2):
            sbuf[g, i] = accp[g, i, :, other].astype(BF16)
        pr(g).start()

    lax.fori_loop(0, heads // 4, own_scores, 0)
    if kv > 1:
        hop(1)
    lax.fori_loop(heads // 4, heads // 2, own_scores, 0)
    forward()
    if kv > 2:
        hop(2)
    if kv > 1:
        relay(1)
    if kv > 3:
        hop(3)

    def advance(b, carry):
        t = b * many
        g = t // group
        r = t % group

        @pl.when(r == 0)
        def _():
            shared(g)

        weigh(t, 0)
        weigh(t + 1, 1)
        collect(t, 0)
        collect(t + 1, 1)

        if kv > 1:
            @pl.when((r == group - many) & (g == 0))
            def _():
                finish(1)

        @pl.when(b + 2 < kv)
        def _():
            relay(b + 2)

        @pl.when(b + 4 < kv)
        def _():
            hop(b + 4)

        @pl.when((r == 0) & (g > 0) & (g + 1 < kv))
        def _():
            finish(g + 1)

        @pl.when((r == 0) & (g > 0))
        def _():
            round_a(g - 1)

        @pl.when((r == 0) & (g > 1))
        def _():
            round_b(g - 2)

        @pl.when(r == group - many)
        def _():
            start_pair(g)

        return carry

    lax.fori_loop(0, heads // many, advance, 0)

    def turn_back(b, carry):
        rows = pl.ds(pl.multiple_of(b * step, step), step)
        dq_ref[rows] = swap(dqt[:, rows, :])
        return carry

    lax.fori_loop(0, kv // 4, late, 0)
    round_a(kv - 1)
    lax.fori_loop(kv // 4, kv // 2, late, 0)
    if kv > 1:
        round_b(kv - 2)
    lax.fori_loop(kv // 2, 3 * kv // 4, late, 0)
    lax.fori_loop(3 * kv // 4, kv, late, 0)
    lax.fori_loop(0, tokens // step, turn_back, 0)
    round_b(kv - 1)
    gks_ref[...] = swap(acco[0])
    gvs_ref[...] = swap(acco[1])
    for g in range(kv):
        for i in range(2):
            accp[g, i, z, c] += rbuf[g, i, z].astype(F32)
        near(g, z // 2).wait_recv()
        for i in range(2):
            accp[g, i, z, c] += rina[g, z // 2, i].astype(F32)
        for k in range(1, n_roll // 2):
            far(g, k).wait_recv()
            for i in range(2):
                accp[g, i, z, c] += rin[g, k, i].astype(F32)
    for i, out in ((0, gpk_ref), (1, gpv_ref)):
        mine = accp[:, i, z, c]
        out[...] = swap((mine * inv_root if i == 0 else mine).astype(BF16))
    all_sent(kvp.at[:, :, c], fw_send)
    all_sent(kvp.at[0, :n_roll - 1, c], al_send)
    if kv > 1:
        @pl.when((z > 0) & (z < n_roll - 1))
        def _():
            all_sent(kvp.at[:kv - 1, :2, c], hop_send)
            all_sent(kvp.at[:kv - 1, :n_roll - 1, c], relay_send)

        @pl.when((z == 0) | (z == n_roll - 1))
        def _():
            all_sent(kvp.at[:kv - 1, :1, c], hop_send)
    all_sent(sbuf, pr_send)
    all_sent(csum.at[:, :n_roll // 2], ra_send)
    if n_roll > 2:
        all_sent(csum.at[:, :n_roll // 2 - 1], rs_send)


def hand_on(*refs):
    moves = [pltpu.make_async_copy(refs[n], refs[5 + n], refs[10].at[n]) for n in range(5)]
    for copy in moves:
        copy.start()
    for copy in moves:
        copy.wait()


def per_device(n_roll, n_sub, queries, rollout_keys, rollout_values, prefix_keys,
               audio_prefix_values, lengths, grad_out):
    here, tokens, heads, width = queries.shape
    kv = rollout_keys.shape[2]
    part = prefix_keys.shape[0]
    prefix = n_roll * n_sub * part
    any_space = pl.BlockSpec(memory_space=pltpu.HBM)
    shapes = (
        (tokens, heads, width), (tokens, kv, width), (tokens, kv, width), (part, kv, width), (part, kv, width),
    )
    results = tuple(jax.ShapeDtypeStruct(shape, BF16) for shape in shapes)
    dma = pltpu.SemaphoreType.DMA
    outs = pl.pallas_call(
        functools.partial(kernel, n_roll, n_sub),
        out_shape=tuple(pltpu.VMEM(shape, BF16) for shape in shapes),
        in_specs=[pl.BlockSpec(memory_space=pltpu.SMEM)] + [any_space] * 6,
        out_specs=(pl.BlockSpec(memory_space=pltpu.VMEM),) * 5,
        scratch_shapes=[
            pltpu.VMEM(shapes[0], BF16), pltpu.VMEM(shapes[1], BF16), pltpu.VMEM(shapes[2], BF16),
            pltpu.VMEM(shapes[3], BF16), pltpu.VMEM(shapes[4], BF16), pltpu.VMEM(shapes[0], BF16),
            pltpu.VMEM((heads, tokens, width), BF16),
            pltpu.VMEM((heads, tokens, width), BF16),
            pltpu.VMEM((kv, n_roll, n_sub, 2, part, width), BF16),
            pltpu.VMEM((kv, 2, tokens, width), BF16),
            pltpu.VMEM((kv, 2, n_roll, n_sub, part, width), F32),
            pltpu.VMEM((2, kv, tokens, width), BF16),
            pltpu.VMEM((heads, tokens, width), BF16),
            pltpu.VMEM((2, prefix, tokens), F32),
            pltpu.VMEM((2, prefix, tokens), F32),
            pltpu.VMEM((2, prefix, tokens), BF16),
            pltpu.VMEM((heads, tokens, tokens), F32),
            pltpu.VMEM((heads, tokens, tokens), F32),
            pltpu.VMEM((heads, tokens // 128, 3, 1, tokens), F32),
            pltpu.VMEM((heads, prefix + tokens, tokens), BF16),
            pltpu.VMEM((heads, tokens, tokens), BF16),
            pltpu.VMEM((kv, 2, n_roll, part, width), BF16),
            pltpu.VMEM((kv, 2, n_roll, part, width), BF16),
            pltpu.VMEM((kv, n_roll, 2, part, width), BF16),
            pltpu.VMEM((kv, n_roll, 2, part, width), BF16),
            pltpu.VMEM((kv, n_roll // 2, 2, part, width), BF16),
            dma, dma, dma, dma((kv, n_roll)),
            dma, dma((kv,)),
            dma, dma((kv,)),
            dma, dma((kv, max(1, n_roll // 2 - 1))),
            dma, dma((kv, n_roll // 2)),
            dma((6,)),
        ],
        compiler_params=pltpu.CompilerParams(
            collective_id=0, has_side_effects=True, vmem_limit_bytes=VMEM_MIB * 1024 * 1024
        ),
    )(lengths, queries[0], rollout_keys[0], rollout_values[0], prefix_keys,
      audio_prefix_values, grad_out[0])
    outs = pl.pallas_call(
        hand_on,
        out_shape=results,
        in_specs=[pl.BlockSpec(memory_space=pltpu.VMEM)] * 5,
        out_specs=(any_space,) * 5,
        scratch_shapes=[dma((5,))],
    )(*[pltpu.with_memory_space_constraint(out, pltpu.VMEM) for out in outs])
    return outs[0][None], outs[1][None], outs[2][None], outs[3], outs[4]


def solution(mesh):
    rows = P(("grp", "roll", "sub"), None, "head", None)
    pieces = P(("grp", "roll", "sub"), "head", None)
    return jax.shard_map(
        functools.partial(per_device, mesh.shape["roll"], mesh.shape["sub"]),
        mesh=mesh,
        in_specs=(rows, rows, rows, pieces, pieces, P(("grp", "roll", "sub")), rows),
        out_specs=(rows, rows, rows, pieces, pieces),
        check_vma=False,
    )
```

```python
import functools
import math

import jax
import jax.numpy as jnp
from jax import lax
from jax.experimental import pallas as pl
from jax.experimental.pallas import tpu as pltpu
from jax.sharding import PartitionSpec as P

MESH = pl.DeviceIdType.MESH
VMEM_MIB = 56
LOG2E = math.log2(math.e)
F32 = jnp.float32
BF16 = jnp.bfloat16


def nt(a, b):
    return lax.dot_general(a, b, (((1,), (1,)), ((), ())), preferred_element_type=F32)


def nn(a, b):
    return lax.dot_general(a, b, (((1,), (0,)), ((), ())), preferred_element_type=F32)


def tn(a, b):
    return lax.dot_general(a, b, (((0,), (0,)), ((), ())), preferred_element_type=F32)


def swap(x):
    return jnp.transpose(x, (1, 0, 2))


def kernel(
    n_roll, n_sub,
    len_ref, q_in, ks_in, vs_in, pk_in, pv_in, do_in,
    dq_ref, gks_ref, gvs_ref, gpk_ref, gpv_ref,
    q_ref, ks_ref, vs_ref, pk_ref, pv_ref, do_ref,
    qt, dot, kvp, kvo, accp, acco, dqt, es, ds, gw, eo, wo, so, ga, wa, sbuf, rbuf, csum, rin, rina,
    al_send, hop_send, relay_send, ag_recv, fw_send, fw_recv, pr_send, pr_recv, rs_send, rs_recv, ra_send, ra_recv, in_sem,
):
    z = lax.axis_index("roll")
    c = lax.axis_index("sub")
    other = 1 - c
    tokens, heads, width = q_ref.shape
    kv = ks_ref.shape[1]
    group = heads // kv
    part = pk_ref.shape[0]
    prefix = n_roll * n_sub * part
    inv_root = 1.0 / math.sqrt(width)

    barrier = pltpu.get_barrier_semaphore()
    for k in range(1, n_roll):
        pl.semaphore_signal(
            barrier, inc=1, device_id={"roll": lax.rem(z + k, n_roll)}, device_id_type=MESH
        )
    pl.semaphore_signal(barrier, inc=1, device_id={"sub": other}, device_id_type=MESH)

    ins = []
    for n, (src, dst) in enumerate((
        (pk_in, pk_ref), (pv_in, pv_ref), (q_in, q_ref), (do_in, do_ref), (ks_in, ks_ref), (vs_in, vs_ref),
    )):
        copy = pltpu.make_async_copy(src, dst, in_sem.at[n])
        copy.start()
        ins.append(copy)

    ins[0].wait()
    pk_t = swap(pk_ref[...])
    ins[1].wait()
    pv_t = swap(pv_ref[...])
    for g in range(kv):
        kvp[g, z, c, 0] = pk_t[g]
        kvp[g, z, c, 1] = pv_t[g]
    pl.semaphore_wait(barrier, n_roll)

    direct = min(2, kv)

    def ag(g, k):
        mine = kvp.at[g, z, c]
        return pltpu.make_async_remote_copy(
            src_ref=mine, dst_ref=mine,
            send_sem=al_send, recv_sem=ag_recv.at[g, z],
            device_id={"roll": lax.rem(z + k, n_roll)}, device_id_type=MESH,
        )

    def offer(g):
        for k in range(1, n_roll):
            ag(g, k).start()
        share(g, z)

    def send_block(g, at, to, sem):
        block = kvp.at[g, at, c]
        return pltpu.make_async_remote_copy(
            src_ref=block, dst_ref=block,
            send_sem=sem, recv_sem=ag_recv.at[g, at],
            device_id={"roll": to}, device_id_type=MESH,
        )

    def all_sent(sent, sem):
        pltpu.make_async_remote_copy(
            src_ref=sent, dst_ref=sent, send_sem=sem, recv_sem=ag_recv.at[0, 0],
            device_id={"sub": other}, device_id_type=MESH,
        ).wait_send()

    def landed(g, at):
        send_block(g, at, z, al_send).wait_recv()

    def hop(g):
        @pl.when(z > 0)
        def _():
            send_block(g, z, z - 1, hop_send).start()

        @pl.when(z < n_roll - 1)
        def _():
            send_block(g, z, z + 1, hop_send).start()

        share(g, z)

    def relay(g):
        @pl.when(z > 0)
        def _():
            landed(g, z - 1)

        @pl.when(z < n_roll - 1)
        def _():
            landed(g, z + 1)

        for to in range(n_roll):
            @pl.when((z >= 1) & (to > z))
            def _():
                send_block(g, z - 1, to, relay_send).start()

            @pl.when((z <= n_roll - 2) & (to < z))
            def _():
                send_block(g, z + 1, to, relay_send).start()

        @pl.when(z > 0)
        def _():
            share(g, z - 1)

        @pl.when(z < n_roll - 1)
        def _():
            share(g, z + 1)

    def finish(g):
        for at in range(n_roll):
            @pl.when((z > at + 1) | (z < at - 1))
            def _():
                landed(g, at)
                share(g, at)

    def fw(g, at):
        block = kvp.at[g, at, c]
        return pltpu.make_async_remote_copy(
            src_ref=block, dst_ref=block,
            send_sem=fw_send, recv_sem=fw_recv.at[g],
            device_id={"sub": other}, device_id_type=MESH,
        )

    def share(g, at):
        fw(g, at).start()

    def shared(g):
        column = kvp.at[g, :, c]
        pltpu.make_async_remote_copy(
            src_ref=column, dst_ref=column,
            send_sem=fw_send, recv_sem=fw_recv.at[g],
            device_id={"sub": other}, device_id_type=MESH,
        ).wait_recv()

    def pr(g):
        return pltpu.make_async_remote_copy(
            src_ref=sbuf.at[g], dst_ref=rbuf.at[g],
            send_sem=pr_send, recv_sem=pr_recv.at[g],
            device_id={"sub": other}, device_id_type=MESH,
        )

    mate = z + 1 - 2 * lax.rem(z, 2)
    side = lax.rem(z, 2)

    def near(g, j):
        return pltpu.make_async_remote_copy(
            src_ref=csum.at[g, 2 * j + 1 - side], dst_ref=rina.at[g, j],
            send_sem=ra_send, recv_sem=ra_recv.at[g, j],
            device_id={"roll": mate}, device_id_type=MESH,
        )

    def far(g, k):
        to = lax.rem(z + 2 * k, n_roll)
        return pltpu.make_async_remote_copy(
            src_ref=csum.at[g, to], dst_ref=rin.at[g, k],
            send_sem=rs_send, recv_sem=rs_recv.at[g, k - 1],
            device_id={"roll": to}, device_id_type=MESH,
        )

    def round_a(g):
        pr(g).wait_recv()
        for n in range(1, n_roll // 2 + 1):
            j = lax.rem(z // 2 + n, n_roll // 2)
            at = 2 * j + 1 - side
            for i in range(2):
                csum[g, at, i] = (accp[g, i, at, c] + rbuf[g, i, at].astype(F32)).astype(BF16)
            near(g, j).start()

    def round_b(g):
        for n in range(1, n_roll // 2):
            near(g, lax.rem(z // 2 + n, n_roll // 2)).wait_recv()
        for k in range(1, n_roll // 2):
            at = lax.rem(z + 2 * k, n_roll)
            for i in range(2):
                csum[g, at, i] = (
                    accp[g, i, at, c] + rbuf[g, i, at].astype(F32) + rina[g, at // 2, i].astype(F32)
                ).astype(BF16)
            far(g, k).start()

    offer(0)

    def forward(g):
        for k in range(1, n_roll):
            at = lax.rem(z + n_roll - k, n_roll)
            landed(g, at)
            share(g, at)

    length = len_ref[0]
    step = 16
    token_at = lax.broadcasted_iota(jnp.int32, (step, heads, width), 0)

    def turn(b, carry):
        at = pl.multiple_of(b * step, step)
        rows = pl.ds(at, step)
        qt[:, rows, :] = swap(q_ref[rows])
        raw = do_ref[rows].astype(F32)
        raw = jnp.where(token_at + at < length, raw, 0.0).astype(BF16)
        dot[:, rows, :] = swap(raw)
        return carry

    ins[2].wait()
    ins[3].wait()
    lax.fori_loop(0, tokens // step, turn, 0)
    ins[4].wait()
    ins[5].wait()
    ks_t = swap(ks_ref[...])
    vs_t = swap(vs_ref[...])
    kvo[:, 0] = ks_t
    kvo[:, 1] = vs_t
    accp[...] = jnp.zeros(accp.shape, F32)

    key_at = lax.broadcasted_iota(jnp.int32, (128, tokens), 0)
    row_at = lax.broadcasted_iota(jnp.int32, (128, tokens), 1)

    scale = inv_root * LOG2E

    tile = 128
    tiles_p = prefix // tile
    tiles_o = tokens // tile

    def tile_stats(s, dp):
        top = jnp.max(s, axis=0, keepdims=True)
        e = jnp.exp2((s - top) * scale)
        return e, top, jnp.sum(e, axis=0, keepdims=True), jnp.sum(e * dp, axis=0, keepdims=True)

    def own_scores(b, carry):
        for m in range(2):
            t = 2 * b + m
            g = t // group
            do = dot[t]
            q = qt[t]
            ko, vo = kvo[g, 0], kvo[g, 1]
            for n in range(tiles_o):
                at = slice(n * tile, (n + 1) * tile)
                s = jnp.where(key_at + n * tile <= row_at, nt(ko[at], q), -1e30)
                dp = nt(vo[at], do)
                e, top, total, inner = tile_stats(s, dp)
                eo[t, at] = e
                wo[t, at] = dp
                so[t, n, 0] = top
                so[t, n, 1] = total
                so[t, n, 2] = inner
        return carry

    def weigh(t, slot):
        g = t // group
        q, do = qt[t], dot[t]
        kp = kvp[g, :, :, 0].reshape(prefix, width)
        vp = kvp[g, :, :, 1].reshape(prefix, width)
        tops, sums, inners = [], [], []
        for n in range(tiles_p):
            at = slice(n * tile, (n + 1) * tile)
            dp = nt(vp[at], do)
            e, top, total, inner = tile_stats(nt(kp[at], q), dp)
            es[slot, at] = e
            ds[slot, at] = dp
            tops.append(top)
            sums.append(total)
            inners.append(inner)
        for n in range(tiles_o):
            tops.append(so[t, n, 0])
            sums.append(so[t, n, 1])
            inners.append(so[t, n, 2])
        most = functools.reduce(jnp.maximum, tops)
        parts = [jnp.exp2((top - most) * scale) for top in tops]
        total = sum(p * x for p, x in zip(parts, sums))
        inner = sum(p * x for p, x in zip(parts, inners))
        inv = 1.0 / total
        delta = inner * inv
        for n in range(tiles_p):
            at = slice(n * tile, (n + 1) * tile)
            w = es[slot, at] * (parts[n] * inv)
            gp = (w * (ds[slot, at] - delta)).astype(BF16)
            ga[t, at] = gp
            gw[slot, at] = w.astype(BF16)
        for n in range(tiles_o):
            so[t, n, 0] = parts[tiles_p + n] * inv
        so[t, 0, 1] = delta

    def collect(t, slot):
        g = t // group
        accp[g, 0] += nn(ga[t, :prefix], qt[t]).reshape(n_roll, n_sub, part, width)
        accp[g, 1] += nn(gw[slot], dot[t]).reshape(n_roll, n_sub, part, width)

    def late(g, carry):
        kp = kvp[g, :, :, 0].reshape(prefix, width)
        ko = kvo[g, 0]
        grad_k = jnp.zeros((tokens, width), F32)
        grad_v = jnp.zeros((tokens, width), F32)
        for m in range(group):
            t = g * group + m
            delta = so[t, 0, 1]
            for n in range(tiles_o):
                at = slice(n * tile, (n + 1) * tile)
                w = eo[t, at] * so[t, n, 0]
                ga[t, prefix + n * tile:prefix + (n + 1) * tile] = (w * (wo[t, at] - delta)).astype(BF16)
                wa[t, at] = w.astype(BF16)
            go = ga[t, prefix:]
            dqt[t] = ((tn(ga[t, :prefix], kp) + tn(go, ko)) * inv_root).astype(BF16)
            grad_k = grad_k + nn(go, qt[t])
            grad_v = grad_v + nn(wa[t], dot[t])
        acco[0, g] = (grad_k * inv_root).astype(BF16)
        acco[1, g] = grad_v.astype(BF16)
        return carry

    many = 2

    def start_pair(g):
        for i in range(2):
            sbuf[g, i] = accp[g, i, :, other].astype(BF16)
        pr(g).start()

    lax.fori_loop(0, heads // 4, own_scores, 0)
    if kv > 2:
        hop(2)
    if kv > 1:
        offer(1)
    lax.fori_loop(heads // 4, heads // 2, own_scores, 0)
    forward(0)

    def advance(b, carry):
        t = b * many
        g = t // group
        r = t % group

        @pl.when(r == 0)
        def _():
            shared(g)

        weigh(t, 0)
        weigh(t + 1, 1)
        collect(t, 0)
        collect(t + 1, 1)

        if kv > 1:
            @pl.when((r == group - many) & (g == 0))
            def _():
                forward(1)

        @pl.when((b >= 1) & (b + 1 < kv))
        def _():
            relay(b + 1)

        @pl.when(b + 3 < kv)
        def _():
            hop(b + 3)

        @pl.when((r == 0) & (g > 0) & (g + 1 < kv))
        def _():
            finish(g + 1)

        @pl.when((r == 0) & (g > 0))
        def _():
            round_a(g - 1)

        @pl.when((r == group - many) & (g > 1))
        def _():
            round_b(g - 2)

        @pl.when(r == group - many)
        def _():
            start_pair(g)

        return carry

    lax.fori_loop(0, heads // many, advance, 0)

    def turn_back(b, carry):
        rows = pl.ds(pl.multiple_of(b * step, step), step)
        dq_ref[rows] = swap(dqt[:, rows, :])
        return carry

    lax.fori_loop(0, kv // 4, late, 0)
    round_a(kv - 1)
    lax.fori_loop(kv // 4, kv // 2, late, 0)
    if kv > 1:
        round_b(kv - 2)
    lax.fori_loop(kv // 2, 3 * kv // 4, late, 0)
    lax.fori_loop(3 * kv // 4, kv, late, 0)
    lax.fori_loop(0, tokens // step, turn_back, 0)
    round_b(kv - 1)
    gks_ref[...] = swap(acco[0])
    gvs_ref[...] = swap(acco[1])
    for g in range(kv):
        for i in range(2):
            accp[g, i, z, c] += rbuf[g, i, z].astype(F32)
        near(g, z // 2).wait_recv()
        for i in range(2):
            accp[g, i, z, c] += rina[g, z // 2, i].astype(F32)
        for k in range(1, n_roll // 2):
            far(g, k).wait_recv()
            for i in range(2):
                accp[g, i, z, c] += rin[g, k, i].astype(F32)
    for i, out in ((0, gpk_ref), (1, gpv_ref)):
        mine = accp[:, i, z, c]
        out[...] = swap((mine * inv_root if i == 0 else mine).astype(BF16))
    all_sent(kvp.at[:, :, c], fw_send)
    all_sent(kvp.at[:direct, :n_roll - 1, c], al_send)
    if kv > direct:
        @pl.when((z > 0) & (z < n_roll - 1))
        def _():
            all_sent(kvp.at[:kv - direct, :2, c], hop_send)
            all_sent(kvp.at[:kv - direct, :n_roll - 1, c], relay_send)

        @pl.when((z == 0) | (z == n_roll - 1))
        def _():
            all_sent(kvp.at[:kv - direct, :1, c], hop_send)
    all_sent(sbuf, pr_send)
    all_sent(csum.at[:, :n_roll // 2], ra_send)
    if n_roll > 2:
        all_sent(csum.at[:, :n_roll // 2 - 1], rs_send)


def hand_on(*refs):
    moves = [pltpu.make_async_copy(refs[n], refs[5 + n], refs[10].at[n]) for n in range(5)]
    for copy in moves:
        copy.start()
    for copy in moves:
        copy.wait()


def per_device(n_roll, n_sub, queries, rollout_keys, rollout_values, prefix_keys,
               audio_prefix_values, lengths, grad_out):
    here, tokens, heads, width = queries.shape
    kv = rollout_keys.shape[2]
    part = prefix_keys.shape[0]
    prefix = n_roll * n_sub * part
    any_space = pl.BlockSpec(memory_space=pltpu.HBM)
    shapes = (
        (tokens, heads, width), (tokens, kv, width), (tokens, kv, width), (part, kv, width), (part, kv, width),
    )
    results = tuple(jax.ShapeDtypeStruct(shape, BF16) for shape in shapes)
    dma = pltpu.SemaphoreType.DMA
    outs = pl.pallas_call(
        functools.partial(kernel, n_roll, n_sub),
        out_shape=tuple(pltpu.VMEM(shape, BF16) for shape in shapes),
        in_specs=[pl.BlockSpec(memory_space=pltpu.SMEM)] + [any_space] * 6,
        out_specs=(pl.BlockSpec(memory_space=pltpu.VMEM),) * 5,
        scratch_shapes=[
            pltpu.VMEM(shapes[0], BF16), pltpu.VMEM(shapes[1], BF16), pltpu.VMEM(shapes[2], BF16),
            pltpu.VMEM(shapes[3], BF16), pltpu.VMEM(shapes[4], BF16), pltpu.VMEM(shapes[0], BF16),
            pltpu.VMEM((heads, tokens, width), BF16),
            pltpu.VMEM((heads, tokens, width), BF16),
            pltpu.VMEM((kv, n_roll, n_sub, 2, part, width), BF16),
            pltpu.VMEM((kv, 2, tokens, width), BF16),
            pltpu.VMEM((kv, 2, n_roll, n_sub, part, width), F32),
            pltpu.VMEM((2, kv, tokens, width), BF16),
            pltpu.VMEM((heads, tokens, width), BF16),
            pltpu.VMEM((2, prefix, tokens), F32),
            pltpu.VMEM((2, prefix, tokens), F32),
            pltpu.VMEM((2, prefix, tokens), BF16),
            pltpu.VMEM((heads, tokens, tokens), F32),
            pltpu.VMEM((heads, tokens, tokens), F32),
            pltpu.VMEM((heads, tokens // 128, 3, 1, tokens), F32),
            pltpu.VMEM((heads, prefix + tokens, tokens), BF16),
            pltpu.VMEM((heads, tokens, tokens), BF16),
            pltpu.VMEM((kv, 2, n_roll, part, width), BF16),
            pltpu.VMEM((kv, 2, n_roll, part, width), BF16),
            pltpu.VMEM((kv, n_roll, 2, part, width), BF16),
            pltpu.VMEM((kv, n_roll, 2, part, width), BF16),
            pltpu.VMEM((kv, n_roll // 2, 2, part, width), BF16),
            dma, dma, dma, dma((kv, n_roll)),
            dma, dma((kv,)),
            dma, dma((kv,)),
            dma, dma((kv, max(1, n_roll // 2 - 1))),
            dma, dma((kv, n_roll // 2)),
            dma((6,)),
        ],
        compiler_params=pltpu.CompilerParams(
            collective_id=0, has_side_effects=True, vmem_limit_bytes=VMEM_MIB * 1024 * 1024
        ),
    )(lengths, queries[0], rollout_keys[0], rollout_values[0], prefix_keys,
      audio_prefix_values, grad_out[0])
    outs = pl.pallas_call(
        hand_on,
        out_shape=results,
        in_specs=[pl.BlockSpec(memory_space=pltpu.VMEM)] * 5,
        out_specs=(any_space,) * 5,
        scratch_shapes=[dma((5,))],
    )(*[pltpu.with_memory_space_constraint(out, pltpu.VMEM) for out in outs])
    return outs[0][None], outs[1][None], outs[2][None], outs[3], outs[4]


def solution(mesh):
    rows = P(("grp", "roll", "sub"), None, "head", None)
    pieces = P(("grp", "roll", "sub"), "head", None)
    return jax.shard_map(
        functools.partial(per_device, mesh.shape["roll"], mesh.shape["sub"]),
        mesh=mesh,
        in_specs=(rows, rows, rows, pieces, pieces, P(("grp", "roll", "sub")), rows),
        out_specs=(rows, rows, rows, pieces, pieces),
        check_vma=False,
    )
```

```python
import functools
import math

import jax
import jax.numpy as jnp
from jax import lax
from jax.experimental import pallas as pl
from jax.experimental.pallas import tpu as pltpu
from jax.sharding import PartitionSpec as P

MESH = pl.DeviceIdType.MESH
VMEM_MIB = 56
LOG2E = math.log2(math.e)
F32 = jnp.float32
BF16 = jnp.bfloat16


def nt(a, b):
    return lax.dot_general(a, b, (((1,), (1,)), ((), ())), preferred_element_type=F32)


def nn(a, b):
    return lax.dot_general(a, b, (((1,), (0,)), ((), ())), preferred_element_type=F32)


def tn(a, b):
    return lax.dot_general(a, b, (((0,), (0,)), ((), ())), preferred_element_type=F32)


def swap(x):
    return jnp.transpose(x, (1, 0, 2))


def kernel(
    n_roll, n_sub,
    len_ref, q_in, ks_in, vs_in, pk_in, pv_in, do_in,
    dq_ref, gks_ref, gvs_ref, gpk_ref, gpv_ref,
    q_ref, ks_ref, vs_ref, pk_ref, pv_ref, do_ref,
    qt, dot, kvp, kvo, accp, acco, dqt, es, ds, gw, eo, wo, so, ga, wa, sbuf, rbuf, csum, rin, rina,
    al_send, hop_send, relay_send, ag_recv, fw_send, fw_recv, pr_send, pr_recv, rs_send, rs_recv, ra_send, ra_recv, in_sem,
):
    z = lax.axis_index("roll")
    c = lax.axis_index("sub")
    other = 1 - c
    tokens, heads, width = q_ref.shape
    kv = ks_ref.shape[1]
    group = heads // kv
    part = pk_ref.shape[0]
    prefix = n_roll * n_sub * part
    inv_root = 1.0 / math.sqrt(width)

    barrier = pltpu.get_barrier_semaphore()
    for k in range(1, n_roll):
        pl.semaphore_signal(
            barrier, inc=1, device_id={"roll": lax.rem(z + k, n_roll)}, device_id_type=MESH
        )
    pl.semaphore_signal(barrier, inc=1, device_id={"sub": other}, device_id_type=MESH)

    ins = []
    for n, (src, dst) in enumerate((
        (pk_in, pk_ref), (pv_in, pv_ref), (q_in, q_ref), (do_in, do_ref), (ks_in, ks_ref), (vs_in, vs_ref),
    )):
        copy = pltpu.make_async_copy(src, dst, in_sem.at[n])
        copy.start()
        ins.append(copy)

    ins[0].wait()
    pk_t = swap(pk_ref[...])
    ins[1].wait()
    pv_t = swap(pv_ref[...])
    for g in range(kv):
        kvp[g, z, c, 0] = pk_t[g]
        kvp[g, z, c, 1] = pv_t[g]
    pl.semaphore_wait(barrier, n_roll)

    direct = min(2, kv)

    def ag(g, k):
        mine = kvp.at[g, z, c]
        return pltpu.make_async_remote_copy(
            src_ref=mine, dst_ref=mine,
            send_sem=al_send, recv_sem=ag_recv.at[g, z],
            device_id={"roll": lax.rem(z + k, n_roll)}, device_id_type=MESH,
        )

    def offer(g):
        for k in range(1, n_roll):
            ag(g, k).start()
        share(g, z)

    def send_block(g, at, to, sem):
        block = kvp.at[g, at, c]
        return pltpu.make_async_remote_copy(
            src_ref=block, dst_ref=block,
            send_sem=sem, recv_sem=ag_recv.at[g, at],
            device_id={"roll": to}, device_id_type=MESH,
        )

    def all_sent(sent, sem):
        pltpu.make_async_remote_copy(
            src_ref=sent, dst_ref=sent, send_sem=sem, recv_sem=ag_recv.at[0, 0],
            device_id={"sub": other}, device_id_type=MESH,
        ).wait_send()

    def landed(g, at):
        send_block(g, at, z, al_send).wait_recv()

    def hop(g):
        @pl.when(z > 0)
        def _():
            send_block(g, z, z - 1, hop_send).start()

        @pl.when(z < n_roll - 1)
        def _():
            send_block(g, z, z + 1, hop_send).start()

        share(g, z)

    def relay(g):
        @pl.when(z > 0)
        def _():
            landed(g, z - 1)

        @pl.when(z < n_roll - 1)
        def _():
            landed(g, z + 1)

        for to in range(n_roll):
            @pl.when((z >= 1) & (to > z))
            def _():
                send_block(g, z - 1, to, relay_send).start()

            @pl.when((z <= n_roll - 2) & (to < z))
            def _():
                send_block(g, z + 1, to, relay_send).start()

        @pl.when(z > 0)
        def _():
            share(g, z - 1)

        @pl.when(z < n_roll - 1)
        def _():
            share(g, z + 1)

    def finish(g):
        for at in range(n_roll):
            @pl.when((z > at + 1) | (z < at - 1))
            def _():
                landed(g, at)
                share(g, at)

    def fw(g, at):
        block = kvp.at[g, at, c]
        return pltpu.make_async_remote_copy(
            src_ref=block, dst_ref=block,
            send_sem=fw_send, recv_sem=fw_recv.at[g],
            device_id={"sub": other}, device_id_type=MESH,
        )

    def share(g, at):
        fw(g, at).start()

    def shared(g):
        column = kvp.at[g, :, c]
        pltpu.make_async_remote_copy(
            src_ref=column, dst_ref=column,
            send_sem=fw_send, recv_sem=fw_recv.at[g],
            device_id={"sub": other}, device_id_type=MESH,
        ).wait_recv()

    def pr(g):
        return pltpu.make_async_remote_copy(
            src_ref=sbuf.at[g], dst_ref=rbuf.at[g],
            send_sem=pr_send, recv_sem=pr_recv.at[g],
            device_id={"sub": other}, device_id_type=MESH,
        )

    mate = z + 1 - 2 * lax.rem(z, 2)
    side = lax.rem(z, 2)

    def near(g, j):
        return pltpu.make_async_remote_copy(
            src_ref=csum.at[g, 2 * j + 1 - side], dst_ref=rina.at[g, j],
            send_sem=ra_send, recv_sem=ra_recv.at[g, j],
            device_id={"roll": mate}, device_id_type=MESH,
        )

    def far(g, k):
        to = lax.rem(z + 2 * k, n_roll)
        return pltpu.make_async_remote_copy(
            src_ref=csum.at[g, to], dst_ref=rin.at[g, k],
            send_sem=rs_send, recv_sem=rs_recv.at[g, k - 1],
            device_id={"roll": to}, device_id_type=MESH,
        )

    def round_a(g):
        pr(g).wait_recv()
        for n in range(1, n_roll // 2 + 1):
            j = lax.rem(z // 2 + n, n_roll // 2)
            at = 2 * j + 1 - side
            for i in range(2):
                csum[g, at, i] = (accp[g, i, at, c] + rbuf[g, i, at].astype(F32)).astype(BF16)
            near(g, j).start()

    def round_b(g):
        for n in range(1, n_roll // 2):
            near(g, lax.rem(z // 2 + n, n_roll // 2)).wait_recv()
        for k in range(1, n_roll // 2):
            at = lax.rem(z + 2 * k, n_roll)
            for i in range(2):
                csum[g, at, i] = (
                    accp[g, i, at, c] + rbuf[g, i, at].astype(F32) + rina[g, at // 2, i].astype(F32)
                ).astype(BF16)
            far(g, k).start()

    offer(0)

    def forward(g):
        for k in range(1, n_roll):
            at = lax.rem(z + n_roll - k, n_roll)
            landed(g, at)
            share(g, at)

    length = len_ref[0]
    step = 16
    token_at = lax.broadcasted_iota(jnp.int32, (step, heads, width), 0)

    def turn(b, carry):
        at = pl.multiple_of(b * step, step)
        rows = pl.ds(at, step)
        qt[:, rows, :] = swap(q_ref[rows])
        raw = do_ref[rows].astype(F32)
        raw = jnp.where(token_at + at < length, raw, 0.0).astype(BF16)
        dot[:, rows, :] = swap(raw)
        return carry

    ins[2].wait()
    ins[3].wait()
    lax.fori_loop(0, tokens // step, turn, 0)
    ins[4].wait()
    ins[5].wait()
    ks_t = swap(ks_ref[...])
    vs_t = swap(vs_ref[...])
    kvo[:, 0] = ks_t
    kvo[:, 1] = vs_t
    accp[...] = jnp.zeros(accp.shape, F32)

    key_at = lax.broadcasted_iota(jnp.int32, (128, tokens), 0)
    row_at = lax.broadcasted_iota(jnp.int32, (128, tokens), 1)

    scale = inv_root * LOG2E

    tile = 128
    tiles_p = prefix // tile
    tiles_o = tokens // tile

    def tile_stats(s, dp):
        top = jnp.max(s, axis=0, keepdims=True)
        e = jnp.exp2((s - top) * scale)
        return e, top, jnp.sum(e, axis=0, keepdims=True), jnp.sum(e * dp, axis=0, keepdims=True)

    def own_scores(b, carry):
        for m in range(2):
            t = 2 * b + m
            g = t // group
            do = dot[t]
            q = qt[t]
            ko, vo = kvo[g, 0], kvo[g, 1]
            for n in range(tiles_o):
                at = slice(n * tile, (n + 1) * tile)
                s = jnp.where(key_at + n * tile <= row_at, nt(ko[at], q), -1e30)
                dp = nt(vo[at], do)
                e, top, total, inner = tile_stats(s, dp)
                eo[t, at] = e
                wo[t, at] = dp
                so[t, n, 0] = top
                so[t, n, 1] = total
                so[t, n, 2] = inner
        return carry

    def weigh(t, slot):
        g = t // group
        q, do = qt[t], dot[t]
        kp = kvp[g, :, :, 0].reshape(prefix, width)
        vp = kvp[g, :, :, 1].reshape(prefix, width)
        tops, sums, inners = [], [], []
        for n in range(tiles_p):
            at = slice(n * tile, (n + 1) * tile)
            dp = nt(vp[at], do)
            e, top, total, inner = tile_stats(nt(kp[at], q), dp)
            es[slot, at] = e
            ds[slot, at] = dp
            tops.append(top)
            sums.append(total)
            inners.append(inner)
        for n in range(tiles_o):
            tops.append(so[t, n, 0])
            sums.append(so[t, n, 1])
            inners.append(so[t, n, 2])
        most = functools.reduce(jnp.maximum, tops)
        parts = [jnp.exp2((top - most) * scale) for top in tops]
        total = sum(p * x for p, x in zip(parts, sums))
        inner = sum(p * x for p, x in zip(parts, inners))
        inv = 1.0 / total
        delta = inner * inv
        for n in range(tiles_p):
            at = slice(n * tile, (n + 1) * tile)
            w = es[slot, at] * (parts[n] * inv)
            gp = (w * (ds[slot, at] - delta)).astype(BF16)
            ga[t, at] = gp
            gw[slot, at] = w.astype(BF16)
        for n in range(tiles_o):
            so[t, n, 0] = parts[tiles_p + n] * inv
        so[t, 0, 1] = delta

    def collect(t, slot):
        g = t // group
        accp[g, 0] += nn(ga[t, :prefix], qt[t]).reshape(n_roll, n_sub, part, width)
        accp[g, 1] += nn(gw[slot], dot[t]).reshape(n_roll, n_sub, part, width)

    def late(g, carry):
        kp = kvp[g, :, :, 0].reshape(prefix, width)
        ko = kvo[g, 0]
        grad_k = jnp.zeros((tokens, width), F32)
        grad_v = jnp.zeros((tokens, width), F32)
        for m in range(group):
            t = g * group + m
            delta = so[t, 0, 1]
            for n in range(tiles_o):
                at = slice(n * tile, (n + 1) * tile)
                w = eo[t, at] * so[t, n, 0]
                ga[t, prefix + n * tile:prefix + (n + 1) * tile] = (w * (wo[t, at] - delta)).astype(BF16)
                wa[t, at] = w.astype(BF16)
            go = ga[t, prefix:]
            dqt[t] = ((tn(ga[t, :prefix], kp) + tn(go, ko)) * inv_root).astype(BF16)
            grad_k = grad_k + nn(go, qt[t])
            grad_v = grad_v + nn(wa[t], dot[t])
        acco[0, g] = (grad_k * inv_root).astype(BF16)
        acco[1, g] = grad_v.astype(BF16)
        return carry

    many = 2

    def start_pair(g):
        for i in range(2):
            sbuf[g, i] = accp[g, i, :, other].astype(BF16)
        pr(g).start()

    lax.fori_loop(0, heads // 4, own_scores, 0)
    if kv > 2:
        hop(2)
    if kv > 1:
        offer(1)
    lax.fori_loop(heads // 4, heads // 2, own_scores, 0)
    forward(0)

    def advance(b, carry):
        t = b * many
        g = t // group
        r = t % group

        @pl.when(r == 0)
        def _():
            shared(g)

        weigh(t, 0)
        weigh(t + 1, 1)
        collect(t, 0)
        collect(t + 1, 1)

        @pl.when((b >= 1) & (b + 1 < kv))
        def _():
            relay(b + 1)

        if kv > 1:
            @pl.when((r == group - many) & (g == 0))
            def _():
                forward(1)

        @pl.when(b + 3 < kv)
        def _():
            hop(b + 3)

        @pl.when((r == 0) & (g > 0) & (g + 1 < kv))
        def _():
            finish(g + 1)

        @pl.when((r == 0) & (g > 0))
        def _():
            round_a(g - 1)

        @pl.when((r == group - many) & (g > 1))
        def _():
            round_b(g - 2)

        @pl.when(r == group - many)
        def _():
            start_pair(g)

        return carry

    lax.fori_loop(0, heads // many, advance, 0)

    def turn_back(b, carry):
        rows = pl.ds(pl.multiple_of(b * step, step), step)
        dq_ref[rows] = swap(dqt[:, rows, :])
        return carry

    lax.fori_loop(0, kv // 4, late, 0)
    round_a(kv - 1)
    lax.fori_loop(kv // 4, kv // 2, late, 0)
    if kv > 1:
        round_b(kv - 2)
    lax.fori_loop(kv // 2, 3 * kv // 4, late, 0)
    lax.fori_loop(3 * kv // 4, kv, late, 0)
    lax.fori_loop(0, tokens // step, turn_back, 0)
    round_b(kv - 1)
    gks_ref[...] = swap(acco[0])
    gvs_ref[...] = swap(acco[1])
    for g in range(kv):
        for i in range(2):
            accp[g, i, z, c] += rbuf[g, i, z].astype(F32)
        near(g, z // 2).wait_recv()
        for i in range(2):
            accp[g, i, z, c] += rina[g, z // 2, i].astype(F32)
        for k in range(1, n_roll // 2):
            far(g, k).wait_recv()
            for i in range(2):
                accp[g, i, z, c] += rin[g, k, i].astype(F32)
    for i, out in ((0, gpk_ref), (1, gpv_ref)):
        mine = accp[:, i, z, c]
        out[...] = swap((mine * inv_root if i == 0 else mine).astype(BF16))
    all_sent(kvp.at[:, :, c], fw_send)
    all_sent(kvp.at[:direct, :n_roll - 1, c], al_send)
    if kv > direct:
        @pl.when((z > 0) & (z < n_roll - 1))
        def _():
            all_sent(kvp.at[:kv - direct, :2, c], hop_send)
            all_sent(kvp.at[:kv - direct, :n_roll - 1, c], relay_send)

        @pl.when((z == 0) | (z == n_roll - 1))
        def _():
            all_sent(kvp.at[:kv - direct, :1, c], hop_send)
    all_sent(sbuf, pr_send)
    all_sent(csum.at[:, :n_roll // 2], ra_send)
    if n_roll > 2:
        all_sent(csum.at[:, :n_roll // 2 - 1], rs_send)


def hand_on(*refs):
    moves = [pltpu.make_async_copy(refs[n], refs[5 + n], refs[10].at[n]) for n in range(5)]
    for copy in moves:
        copy.start()
    for copy in moves:
        copy.wait()


def per_device(n_roll, n_sub, queries, rollout_keys, rollout_values, prefix_keys,
               audio_prefix_values, lengths, grad_out):
    here, tokens, heads, width = queries.shape
    kv = rollout_keys.shape[2]
    part = prefix_keys.shape[0]
    prefix = n_roll * n_sub * part
    any_space = pl.BlockSpec(memory_space=pltpu.HBM)
    shapes = (
        (tokens, heads, width), (tokens, kv, width), (tokens, kv, width), (part, kv, width), (part, kv, width),
    )
    results = tuple(jax.ShapeDtypeStruct(shape, BF16) for shape in shapes)
    dma = pltpu.SemaphoreType.DMA
    outs = pl.pallas_call(
        functools.partial(kernel, n_roll, n_sub),
        out_shape=tuple(pltpu.VMEM(shape, BF16) for shape in shapes),
        in_specs=[pl.BlockSpec(memory_space=pltpu.SMEM)] + [any_space] * 6,
        out_specs=(pl.BlockSpec(memory_space=pltpu.VMEM),) * 5,
        scratch_shapes=[
            pltpu.VMEM(shapes[0], BF16), pltpu.VMEM(shapes[1], BF16), pltpu.VMEM(shapes[2], BF16),
            pltpu.VMEM(shapes[3], BF16), pltpu.VMEM(shapes[4], BF16), pltpu.VMEM(shapes[0], BF16),
            pltpu.VMEM((heads, tokens, width), BF16),
            pltpu.VMEM((heads, tokens, width), BF16),
            pltpu.VMEM((kv, n_roll, n_sub, 2, part, width), BF16),
            pltpu.VMEM((kv, 2, tokens, width), BF16),
            pltpu.VMEM((kv, 2, n_roll, n_sub, part, width), F32),
            pltpu.VMEM((2, kv, tokens, width), BF16),
            pltpu.VMEM((heads, tokens, width), BF16),
            pltpu.VMEM((2, prefix, tokens), F32),
            pltpu.VMEM((2, prefix, tokens), F32),
            pltpu.VMEM((2, prefix, tokens), BF16),
            pltpu.VMEM((heads, tokens, tokens), F32),
            pltpu.VMEM((heads, tokens, tokens), F32),
            pltpu.VMEM((heads, tokens // 128, 3, 1, tokens), F32),
            pltpu.VMEM((heads, prefix + tokens, tokens), BF16),
            pltpu.VMEM((heads, tokens, tokens), BF16),
            pltpu.VMEM((kv, 2, n_roll, part, width), BF16),
            pltpu.VMEM((kv, 2, n_roll, part, width), BF16),
            pltpu.VMEM((kv, n_roll, 2, part, width), BF16),
            pltpu.VMEM((kv, n_roll, 2, part, width), BF16),
            pltpu.VMEM((kv, n_roll // 2, 2, part, width), BF16),
            dma, dma, dma, dma((kv, n_roll)),
            dma, dma((kv,)),
            dma, dma((kv,)),
            dma, dma((kv, max(1, n_roll // 2 - 1))),
            dma, dma((kv, n_roll // 2)),
            dma((6,)),
        ],
        compiler_params=pltpu.CompilerParams(
            collective_id=0, has_side_effects=True, vmem_limit_bytes=VMEM_MIB * 1024 * 1024
        ),
    )(lengths, queries[0], rollout_keys[0], rollout_values[0], prefix_keys,
      audio_prefix_values, grad_out[0])
    outs = pl.pallas_call(
        hand_on,
        out_shape=results,
        in_specs=[pl.BlockSpec(memory_space=pltpu.VMEM)] * 5,
        out_specs=(any_space,) * 5,
        scratch_shapes=[dma((5,))],
    )(*[pltpu.with_memory_space_constraint(out, pltpu.VMEM) for out in outs])
    return outs[0][None], outs[1][None], outs[2][None], outs[3], outs[4]


def solution(mesh):
    rows = P(("grp", "roll", "sub"), None, "head", None)
    pieces = P(("grp", "roll", "sub"), "head", None)
    return jax.shard_map(
        functools.partial(per_device, mesh.shape["roll"], mesh.shape["sub"]),
        mesh=mesh,
        in_specs=(rows, rows, rows, pieces, pieces, P(("grp", "roll", "sub")), rows),
        out_specs=(rows, rows, rows, pieces, pieces),
        check_vma=False,
    )
```
